32 devices in a mesh: narrow: 4 (over y, x), wide: 8 (over z, core).
Axes of the slice: x: 2, y: 2, z: 4, core: 2. Of those that a mesh axis runs over, the one named last changes fastest.
Arguments:
- level_set: float32 [256, 256, 512], P('wide', 'narrow')
- velocity: bfloat16 [3, 256, 256, 512], P(None, 'wide', 'narrow'), may hold values from -2 to 2
- box_owner: int32 [8, 4, 256, 1], P('wide', 'narrow'), may hold values from 0 to 7; in each aligned block of 256 rows (0 to 255, 256 to 511, ..., all dimensions but the last counted through in order) at most 80 rows name the same one
Outputs:
- surface: float32 [256, 256, 512], P('wide', 'narrow')
- box_fractions: float32 [8, 4, 640, 512], P('wide', 'narrow')
The draws below stay inside these ranges and needn't reach their ends.
Inputs may be any that keep to these rules, and one draw needn't show every extreme that they name: `box_owner`: the tiles of one device name one box owner at most 80 times.
All inputs are finite; a program needn't handle non-finite values.
Results may differ from the reference program's by a relative error of at most 0.0003.
Values sent between devices are 32-bit elements; how exact they have to be, the bound alone decides.
No kernel may reach another device: no remote copies, remote signals or barrier semaphores. Data moves between devices by JAX's collectives and lax.ppermute only.
A program may use at most 192 MiB of HBM per device.

```python
import math
import jax
import jax.numpy as jnp
import numpy as np
from jax import lax

TILE = 16
CX = 32
CY = 64
CZ = 512
SWEEPS = 3
NX = 256
NY = 256
TPD = 256
CAP = 80
N_NARROW = 4
N_WIDE = 8


def draw_level_set(key, part):
    keys = jax.random.split(key, 3)
    phases = jax.random.uniform(keys[0], (4,), jnp.float32, 0.0, 2.0 * math.pi)
    coord_x = jnp.arange(NX, dtype=jnp.float32)[:, None]
    coord_y = jnp.arange(NY, dtype=jnp.float32)[None, :]
    waves = jnp.sin(2.0 * math.pi * coord_x / NX + phases[0]) + jnp.sin(4.0 * math.pi * coord_y / NY + phases[1])
    waves = waves + 0.5 * jnp.sin(2.0 * math.pi * (coord_x / NX + coord_y / NY) * 3.0 + phases[2])
    roughness = jax.random.uniform(keys[1], (NX, NY), jnp.float32, -3.0, 3.0)
    height = CZ * 0.5 + CZ * 0.12 * waves + roughness
    noise = 0.5 * jax.random.normal(keys[2], (NX, NY, CZ), jnp.float32)
    coord_z = jnp.arange(CZ, dtype=jnp.float32)[None, None, :]
    return 4.0 * jnp.tanh((coord_z - height[:, :, None]) / 6.0) + noise


def block_scale(rng, shape, shards, low, high):
    def one(dim, blocks):
        heights = jax.random.uniform(jax.random.fold_in(jax.random.fold_in(rng, 6), dim), (blocks,), jnp.float32, low / len(shards), high / len(shards))
        return jnp.repeat(jnp.exp(heights), shape[dim] // blocks).reshape((-1,) + (1,) * (len(shape) - dim - 1))

    factor_of = one(*shards[0])
    for cut in shards[1:]:
        factor_of = factor_of * one(*cut)
    return factor_of


def shared_out(stream_key, own, number, rows, number_of, top, most, lean):
    ranking = jax.random.permutation(stream_key, number_of)
    packed, ordinary = load_shares(number_of, rows * top, most, lean, True), load_shares(number_of, rows * top, most, lean, False)
    places = jnp.arange(number_of)

    def named(tallies, rotation):
        used = int((tallies > 0).sum())
        fixed = max(1, used // 4)
        shifted = fixed + (places - fixed + rotation * (used - fixed)) % max(1, number_of - fixed)
        return jnp.zeros((number_of,), jnp.int32).at[ranking[jnp.where(places < fixed, places, shifted)]].set(jnp.asarray(tallies, jnp.int32))

    tallies = jnp.where(number % 4 == 0, named(packed, number // 4), named(ordinary, number - number // 4 - 1))
    mixed = jax.random.permutation(jax.random.fold_in(own, 3), number_of)
    source_of, sink = mixed[0:number_of // 2 * 2:2], mixed[1:number_of // 2 * 2:2]
    margin = jnp.minimum(tallies[source_of] - 1, most - tallies[sink]) // 2
    margin = jnp.where((source_of == ranking[0]) | (sink == ranking[0]) | (tallies[sink] == 0), 0, jnp.maximum(margin, 0))
    shifted = jax.random.randint(jax.random.fold_in(own, 4), (number_of // 2,), 0, 1 << 20) % (margin + 1)
    tallies = tallies.at[source_of].add(-shifted).at[sink].add(shifted)
    items = jnp.searchsorted(jnp.cumsum(tallies), jnp.arange(rows * top), side="right").astype(jnp.int32)
    grid = items.reshape(top, rows).T
    grid = grid[jax.random.permutation(jax.random.fold_in(own, 1), rows)]
    rotation = jax.random.randint(jax.random.fold_in(own, 2), (rows, 1), 0, top)
    return jnp.take_along_axis(grid, (jnp.arange(top)[None, :] + rotation) % top, axis=1)


def load_shares(count, total, limit, skew, full):
    loads = [(1 << 20) // math.isqrt(rank ** skew) + 1 for rank in range(1, count + 1)]
    largest = limit if full else min(limit, max(-(-total // count), total * loads[0] // sum(loads)))
    least = 1 if total - largest >= count - 1 else 0
    given, surplus = [largest] + [least] * (count - 1), total - largest - least * (count - 1)
    while surplus > 0:
        candidates = [i for i in range(1, count) if given[i] < largest] or [i for i in range(1, count) if given[i] < limit]
        whole, budget = sum([loads[i] for i in candidates]), surplus
        for i in candidates:
            more = min(limit - given[i], max(1, budget * loads[i] // whole), surplus)
            given[i] = given[i] + more
            surplus = surplus - more
    return np.array(given)


def normal_values(rng, shape, scale, most, pieces=(), kind=jnp.bfloat16):
    values = scale * jax.random.normal(rng, shape, jnp.float32)
    if pieces:
        values = values * block_scale(rng, shape, pieces, -0.22, 0.18)
    return jnp.clip(values, -most, most).astype(kind)


def setup_inputs(seed: int = 0) -> dict:
    arg_keys = jax.random.split(jax.random.key(seed), 4)
    level_set = draw_level_set(jax.random.fold_in(arg_keys[3], 71), 0)
    velocity = normal_values(arg_keys[1], (3, NX, NY, CZ), 0.15, 2.0, ((1, 8), (2, 4)))
    box_owner_keys = jax.random.split(jax.random.fold_in(arg_keys[2], 1), N_WIDE * N_NARROW * TPD // TPD)
    box_owner_turns = jax.random.permutation(jax.random.fold_in(arg_keys[2], 3), N_WIDE * N_NARROW * TPD // TPD)
    box_owner = jax.vmap(lambda own, number: shared_out(jax.random.fold_in(arg_keys[2], 2), own, number, TPD, N_WIDE, 1, CAP, 2))(box_owner_keys, box_owner_turns).reshape((N_WIDE, N_NARROW, TPD, 1))
    return {"level_set": level_set, "velocity": velocity, "box_owner": box_owner}


WENO_EPS = 1e-06
PSEUDO_STEP = 0.3

def weno_blend(parts):
    guesses = (parts[0] / 3.0 - 7.0 * parts[1] / 6.0 + 11.0 * parts[2] / 6.0, -parts[1] / 6.0 + 5.0 * parts[2] / 6.0 + parts[3] / 3.0, parts[2] / 3.0 + 5.0 * parts[3] / 6.0 - parts[4] / 6.0)
    roughness = (13.0 / 12.0 * jnp.square(parts[0] - 2.0 * parts[1] + parts[2]) + 0.25 * jnp.square(parts[0] - 4.0 * parts[1] + 3.0 * parts[2]), 13.0 / 12.0 * jnp.square(parts[1] - 2.0 * parts[2] + parts[3]) + 0.25 * jnp.square(parts[1] - parts[3]), 13.0 / 12.0 * jnp.square(parts[2] - 2.0 * parts[3] + parts[4]) + 0.25 * jnp.square(3.0 * parts[2] - 4.0 * parts[3] + parts[4]))
    weights = [ideal_share / jnp.square(WENO_EPS + rough_part) for ideal_share, rough_part in zip((0.1, 0.6, 0.3), roughness)]
    numerator = weights[0] * guesses[0] + weights[1] * guesses[1] + weights[2] * guesses[2]
    return numerator / (weights[0] + weights[1] + weights[2])

def weno_pair(padded, along):
    extent = padded.shape[along] - 6
    differences = jnp.diff(padded, axis=along)
    stencil = [lax.slice_in_dim(differences, offset, offset + extent, axis=along) for offset in range(6)]
    from_below = weno_blend(stencil[0:5])
    from_above = weno_blend([stencil[5], stencil[4], stencil[3], stencil[2], stencil[1]])
    return (from_below, from_above)

def upwind(padded, along, speed):
    from_below, from_above = weno_pair(padded, along)
    return speed * jnp.where(speed > 0, from_below, from_above)

def advect_from(field, along_x, along_y, along_z, velocity):
    speeds = velocity.astype(jnp.float32)
    change = upwind(along_x, 0, speeds[0]) + upwind(along_y, 1, speeds[1]) + upwind(along_z, 2, speeds[2])
    return field - change

def godunov_sweep(rimmed, initial):
    center = rimmed[1:-1, 1:-1, :]
    column_pad = jnp.pad(center, ((0, 0), (0, 0), (1, 1)), mode='edge')
    smooth_sign = initial / jnp.sqrt(initial * initial + 1.0)
    outside = initial > 0

    def godunov(lower_side, upper_side):
        behind = center - lower_side
        forward = upper_side - center
        outer_term = jnp.maximum(jnp.square(jnp.maximum(behind, 0.0)), jnp.square(jnp.minimum(forward, 0.0)))
        inner_term = jnp.maximum(jnp.square(jnp.minimum(behind, 0.0)), jnp.square(jnp.maximum(forward, 0.0)))
        return jnp.where(outside, outer_term, inner_term)
    squared = godunov(rimmed[:-2, 1:-1, :], rimmed[2:, 1:-1, :])
    squared = squared + godunov(rimmed[1:-1, :-2, :], rimmed[1:-1, 2:, :])
    squared = squared + godunov(column_pad[:, :, :-2], column_pad[:, :, 2:])
    return center - PSEUDO_STEP * smooth_sign * (jnp.sqrt(squared) - 1.0)

def fraction(field):
    return 0.5 - 0.5 * field / jnp.sqrt(field * field + 1.0)

def to_tiles(one_block, edge):
    sizes_a, sizes_b, sizes_c = one_block.shape
    grouped = one_block.reshape(sizes_a // edge, edge, sizes_b // edge, edge, sizes_c // edge, edge)
    return grouped.transpose(0, 2, 4, 1, 3, 5).reshape(-1, edge ** 3)

def restrict(tiles, edge):
    leading = tiles.shape[:-1]
    half_edge = edge // 2
    depth = len(leading)
    grouped = tiles.reshape(leading + (half_edge, 2, half_edge, 2, half_edge, 2))
    return lax.optimization_barrier(jnp.mean(grouped, axis=(depth + 1, depth + 3, depth + 5))).reshape(leading + (half_edge ** 3,))

def pack_matrix(one_route, owners, capacity):
    owners_list = jnp.arange(owners, dtype=jnp.int32)
    matches = (one_route[:, None] == owners_list[None, :]).astype(jnp.int32)
    earlier = jnp.cumsum(matches, axis=0) - matches
    position = lax.optimization_barrier(jnp.sum(earlier * matches, axis=1))
    target = one_route * capacity + position
    targets = jnp.arange(owners * capacity, dtype=jnp.int32)
    return (targets[:, None] == target[None, :]).astype(jnp.float32)

def reference(level_set, velocity, box_owner):
    along_x = jnp.pad(level_set, ((3, 3), (0, 0), (0, 0)), mode='wrap')
    along_y = jnp.pad(level_set, ((0, 0), (3, 3), (0, 0)), mode='wrap')
    along_z = jnp.pad(level_set, ((0, 0), (0, 0), (3, 3)), mode='edge')
    moved = advect_from(level_set, along_x, along_y, along_z, velocity)
    surface = moved
    for sweep_index in range(SWEEPS):
        rimmed = jnp.pad(surface, ((1, 1), (1, 1), (0, 0)), mode='wrap')
        surface = godunov_sweep(rimmed, moved)
    liquid = fraction(surface)
    device_blocks = liquid.reshape(N_WIDE, CX, N_NARROW, CY, CZ).transpose(0, 2, 1, 3, 4)
    device_blocks = device_blocks.reshape(N_WIDE * N_NARROW, CX, CY, CZ)
    routes_flat = box_owner.reshape(N_WIDE * N_NARROW, TPD).astype(jnp.int32)

    def per_device(pair):
        one_block, one_route = pair
        coarse = restrict(to_tiles(one_block, TILE), TILE)
        matrix = pack_matrix(one_route, N_WIDE, CAP)
        return jnp.dot(matrix, coarse, precision=lax.Precision.HIGHEST, preferred_element_type=jnp.float32)
    outgoing = lax.map(per_device, (device_blocks, routes_flat))
    outgoing = outgoing.reshape(N_WIDE, N_NARROW, N_WIDE, CAP, (TILE // 2) ** 3)
    box_fractions = outgoing.transpose(2, 1, 0, 3, 4).reshape(N_WIDE, N_NARROW, N_WIDE * CAP, (TILE // 2) ** 3)
    return (surface, box_fractions)
```

```python
import functools
import math
import jax
import jax.numpy as jnp
import numpy as np
from jax import lax
from jax.experimental import pallas as pl
from jax.experimental.pallas import tpu as pltpu
from jax.sharding import PartitionSpec as P

TILE = 16
SWEEPS = 3
WENO_EPS = 1e-06
PSEUDO_STEP = 0.3
RIM = 3
LANES = 128
ROWS = 8
MIB = 1024 * 1024
VMEM_LIMIT = 47 * MIB


def correction(s1, s2, s3, h1, h0):
    r1 = 1.0 / s1
    r2 = 1.0 / s2
    r3 = 1.0 / s3
    w1 = (r1 * r1) * (1.0 / 3.0)
    w2 = (r2 * r2) * 2.0
    w3 = r3 * r3
    return (w1 * (4.0 * h1 - h0) + (w3 - w2) * h0) / ((w1 + w3) + w2)


def pair_forms(x, y, t):
    t2 = t + t
    q = t * t + 0.75 * WENO_EPS
    y75 = 0.75 * y
    w = q + y75 * x
    u = w + y75 * t2
    v = w - (0.75 * x) * t2
    return u, w, v


def rolled(chunks, shift, fill):
    lane = lax.broadcasted_iota(jnp.int32, chunks[0].shape, 1)
    turned = [pltpu.roll(c, (-shift) % LANES, 1) for c in chunks]
    out = []
    n = len(chunks)
    for k in range(n):
        other = k + (1 if shift > 0 else -1)
        beyond = turned[other] if 0 <= other < n else fill(k)
        mask = lane >= LANES - shift if shift > 0 else lane < -shift
        out.append(jnp.where(mask, beyond, turned[k]))
    return out


def along_z_kernel(core, u_hbm, field, acc, u, uz, sem):
    nx, ny, nz = core.shape
    copies = Copies(sem)
    bounds = [0, nx // 16, nx // 4, nx // 2, 3 * nx // 4, nx]
    groups = list(zip(bounds, bounds[1:]))
    for x0, x1 in groups:
        xs = pl.ds(x0, x1 - x0)
        for k, lanes in lane_chunks(nz):
            copies.start(x0, core.at[xs, :, lanes], field.at[pl.ds(x0 + RIM, x1 - x0), k, pl.ds(ROWS, ny), :])
        copies.start(x0, u_hbm.at[2, xs], uz.at[xs])
    copies.start("u", u_hbm.at[pl.ds(0, 2)], u)
    for x0, x1 in groups:
        copies.wait(x0)
        lax.fori_loop(x0, x1, functools.partial(z_plane, field, uz, acc, ny, nz), 0)
    copies.finish()


def z_plane(field, uz, acc, rows, depth, x, carry):
    n = depth // LANES
    zero = jnp.zeros((ROWS, LANES), jnp.float32)
    eps = 0.75 * WENO_EPS
    for yb in range(rows // ROWS):
        ys = pl.ds(yb * ROWS, ROWS)
        yf = pl.ds(yb * ROWS + ROWS, ROWS)
        f = [field[x + RIM, k, yf, :] for k in range(n)]
        fp = rolled(f, 1, lambda k: f[k])
        fm = rolled(f, -1, lambda k: f[k])
        e = [(fp[k] - f[k]) - (f[k] - fm[k]) for k in range(n)]
        ep = rolled(e, 1, lambda k: zero)
        em = rolled(e, -1, lambda k: zero)
        epp = rolled(e, 2, lambda k: zero)
        emm = rolled(e, -2, lambda k: zero)
        for k in range(n):
            v = uz[x, ys, pl.ds(k * LANES, LANES)].astype(jnp.float32)
            up = v > 0
            c = e[k]
            a = jnp.where(up, emm[k], epp[k])
            b = jnp.where(up, em[k], ep[k])
            d = jnp.where(up, ep[k], em[k])
            al, be, ga = b - a, c - b, d - c
            b75, c75 = 0.75 * b, 0.75 * c
            s1 = (al * al + eps) + b75 * (b + al)
            s2 = (be * be + eps) + b75 * c
            s3 = (ga * ga + eps) + c75 * (c - ga)
            phi = correction(s1, s2, s3, be - al, ga - be)
            mid = 6.0 * (fp[k] - fm[k]) - (ep[k] - em[k])
            v12 = v * (1.0 / 12.0)
            acc[x + RIM, k, yf, :] = f[k] - (v12 * mid - jnp.abs(v12) * phi)
    return carry


def in_vmem(shape, dtype=jnp.float32):
    return pltpu.VMEM(shape, dtype)


def rimmed(shape):
    nx, ny, nz = shape
    return in_vmem((nx + 2 * RIM, nz // LANES, ny + 2 * ROWS, LANES))


def along_z(level_set, velocity):
    nx, ny, nz = level_set.shape
    return pl.pallas_call(
        along_z_kernel,
        in_specs=[ANY, ANY],
        out_specs=[INSIDE] * 3,
        out_shape=[rimmed(level_set.shape)] * 2 + [in_vmem((2, nx, ny, nz), velocity.dtype)],
        scratch_shapes=[pltpu.VMEM((nx, ny, nz), velocity.dtype), pltpu.SemaphoreType.DMA((40,))],
        name="along_z",
        cost_estimate=estimate(level_set, 60),
        compiler_params=pltpu.CompilerParams(vmem_limit_bytes=46 * MIB),
    )(level_set, velocity)


def estimate(block, flops):
    return pl.CostEstimate(flops=flops * block.size, bytes_accessed=8 * block.size, transcendentals=4 * block.size)


class Copies:
    def __init__(self, sem):
        self.sem, self.used, self.groups = sem, 0, {}

    def start(self, group, src, dst):
        copy = pltpu.make_async_copy(src, dst, self.sem.at[self.used])
        self.used += 1
        copy.start()
        self.groups.setdefault(group, []).append(copy)

    def wait(self, group):
        for copy in self.groups.pop(group, ()):
            copy.wait()

    def finish(self):
        for group in list(self.groups):
            self.wait(group)


def lane_chunks(nz):
    return [(k, pl.ds(k * LANES, LANES)) for k in range(nz // LANES)]


def x_column(field, u, acc, k, yb, ranges):
    ys = pl.ds(pl.multiple_of(yb * ROWS, ROWS), ROWS)
    yf = pl.ds(pl.multiple_of(yb * ROWS + ROWS, ROWS), ROWS)
    lanes = pl.ds(pl.multiple_of(k * LANES, LANES), LANES)
    for first, last in ranges:
        f, g, e, t, h, pu, pw, pv = {}, {}, {}, {}, {}, {}, {}, {}

        def value(x):
            f[x] = field[x + RIM, k, yf, :]
            if x - 1 in f:
                g[x - 1] = f[x] - f[x - 1]
            if x - 2 in g:
                e[x - 1] = g[x - 1] - g[x - 2]
            if x - 2 in e:
                t[x - 2] = e[x - 1] - e[x - 2]
                pu[x - 2], pw[x - 2], pv[x - 2] = pair_forms(e[x - 2], e[x - 1], t[x - 2])
            if x - 3 in t:
                h[x - 2] = t[x - 2] - t[x - 3]

        for x in range(first - RIM, first + RIM):
            value(x)
        for x in range(first, last):
            value(x + RIM)
            v = u[0, x, ys, lanes].astype(jnp.float32)
            up = v > 0
            s1 = jnp.where(up, pu[x - 2], pv[x + 1])
            s2 = jnp.where(up, pw[x - 1], pw[x])
            s3 = jnp.where(up, pv[x], pu[x - 1])
            h1 = jnp.where(up, h[x - 1], h[x + 1])
            phi = correction(s1, s2, s3, h1, h[x])
            mid = 6.0 * (g[x] + g[x - 1]) - (e[x + 1] - e[x - 1])
            v12 = v * (1.0 / 12.0)
            acc[x + RIM, k, yf, :] = acc[x + RIM, k, yf, :] - (v12 * mid - jnp.abs(v12) * phi)


def y_plane(field, u, acc, streams, x, n, ranges):
    es, us, ws, vs, hs = streams
    for k in range(n):
        lanes = pl.ds(k * LANES, LANES)

        def at(y):
            return field[x + RIM, k, pl.ds(ROWS + y, ROWS), :]

        for first, last in ranges:
            for b in range(first, last + 1):
                y = b * ROWS - 2
                f0 = at(y)
                es[k, pl.ds(ROWS + b * ROWS, ROWS), :] = (at(y + 1) - f0) - (f0 - at(y - 1))
            for b in range(first, last + 1):
                r = ROWS + b * ROWS
                e0, e1, e_1 = es[k, pl.ds(r, ROWS), :], es[k, pl.ds(r + 1, ROWS), :], es[k, pl.ds(r - 1, ROWS), :]
                t = e1 - e0
                us[k, pl.ds(r, ROWS), :], ws[k, pl.ds(r, ROWS), :], vs[k, pl.ds(r, ROWS), :] = pair_forms(e0, e1, t)
                hs[k, pl.ds(r, ROWS), :] = t - (e0 - e_1)
            for b in range(first, last):
                ys, yf = pl.ds(b * ROWS, ROWS), pl.ds(b * ROWS + ROWS, ROWS)

                def of(ref, d):
                    return ref[k, pl.ds(ROWS + b * ROWS + 2 + d, ROWS), :]

                v = u[1, x, ys, lanes].astype(jnp.float32)
                up = v > 0
                s1 = jnp.where(up, of(us, -2), of(vs, 1))
                s2 = jnp.where(up, of(ws, -1), of(ws, 0))
                s3 = jnp.where(up, of(vs, 0), of(us, -1))
                h1 = jnp.where(up, of(hs, -1), of(hs, 1))
                phi = correction(s1, s2, s3, h1, of(hs, 0))
                mid = 6.0 * (at(b * ROWS + 1) - at(b * ROWS - 1)) - (of(es, 1) - of(es, -1))
                v12 = v * (1.0 / 12.0)
                acc[x + RIM, k, yf, :] = acc[x + RIM, k, yf, :] - (v12 * mid - jnp.abs(v12) * phi)


def place_rows(field, x0, count, n, upper, first, second, ny, at=(0, 0)):
    def body(i, carry):
        for k in range(n):
            lanes = pl.ds(k * LANES, LANES)
            one = first[i, pl.ds(at[0], RIM), lanes]
            two = second[i, pl.ds(at[1], RIM), lanes]
            field[i + x0, k, pl.ds(ROWS - RIM, RIM), :] = jnp.where(upper, two, one)
            field[i + x0, k, pl.ds(ROWS + ny, RIM), :] = jnp.where(upper, one, two)
        return carry

    lax.fori_loop(0, count, body, 0)


def first_is_above(axis):
    return lax.rem(lax.axis_index(axis), 2) == 0


def face_starts(nx):
    even = first_is_above("wide")
    faces = (jnp.where(even, nx - RIM, 0), jnp.where(even, 0, nx - RIM))
    rims = (jnp.where(even, nx + RIM, 0), jnp.where(even, 0, nx + RIM))
    return faces, rims


def pieces(nx):
    count = math.gcd(nx, 4)
    return [(i * (nx // count), nx // count) for i in range(count)]


def edge_rows_kernel(
    field_in, acc_in, u, xa, xb, ya_hbm, yb_hbm, field, acc, yfa_hbm, yfb_hbm, es, us, ws, vs, hs, ya, yb, yf_a, yf_b, sem
):
    _, nx, ny, nz = u.shape
    n, nb = nz // LANES, ny // ROWS
    copies = Copies(sem)
    streams = (es, us, ws, vs, hs)
    _, rims = face_starts(nx)
    upper = first_is_above("narrow")
    for block, rim in zip((xa, xb), rims):
        for k, lanes in lane_chunks(nz):
            copies.start("x", block.at[:, :, lanes], field.at[pl.ds(rim, RIM), k, pl.ds(ROWS, ny), :])
    copies.start("y", ya_hbm, ya)
    copies.start("y", yb_hbm, yb)
    copies.wait("x")

    def edge_column(i, carry):
        x_column(field, u, acc, lax.rem(i, n), lax.div(i, n) * (nb - 1), ((0, nx),))
        return carry

    lax.fori_loop(0, 2 * n, edge_column, 0)
    copies.wait("y")
    place_rows(field, RIM, nx, n, upper, ya, yb, ny)

    def edge_plane(x, carry):
        y_plane(field, u, acc, streams, x, n, ((0, 1), (nb - 1, nb)))
        for k, lanes in lane_chunks(nz):
            lo, hi = acc[x + RIM, k, pl.ds(ROWS, RIM), :], acc[x + RIM, k, pl.ds(ROWS + ny - RIM, RIM), :]
            yf_a[x, :, lanes] = jnp.where(upper, hi, lo)
            yf_b[x, :, lanes] = jnp.where(upper, lo, hi)
        return carry

    for x0, count in pieces(nx):
        xs = pl.ds(x0, count)
        lax.fori_loop(x0, x0 + count, edge_plane, 0)
        copies.start("out", yf_a.at[xs], yfa_hbm.at[xs])
        copies.start("out", yf_b.at[xs], yfb_hbm.at[xs])
    copies.finish()


def edge_planes_kernel(acc_in, field, u, acc, bx_a, bx_b, es, us, ws, vs, hs, sem):
    _, nx, ny, nz = u.shape
    n, nb = nz // LANES, ny // ROWS
    copies = Copies(sem)
    faces, _ = face_starts(nx)

    def both_ends(i, carry):
        y_plane(field, u, acc, (es, us, ws, vs, hs), jnp.where(i < RIM, i, nx - 2 * RIM + i), n, ((1, nb - 1),))
        return carry

    lax.fori_loop(0, 2 * RIM, both_ends, 0)

    def inner_column(i, carry):
        x_column(field, u, acc, lax.rem(i, n), 1 + lax.div(i, n), ((0, RIM), (nx - RIM, nx)))
        return carry

    lax.fori_loop(0, n * (nb - 2), inner_column, 0)
    rows = pl.ds(ROWS, ny)
    for face, out in zip(faces, (bx_a, bx_b)):
        for k, lanes in lane_chunks(nz):
            copies.start("out", acc.at[pl.ds(face + RIM, RIM), k, rows, :], out.at[:, rows, lanes])
    copies.finish()


def interior_kernel(acc_in, field, u, after, acc, es, us, ws, vs, hs):
    _, nx, ny, nz = u.shape
    n, nb = nz // LANES, ny // ROWS

    def rows(x, carry):
        y_plane(field, u, acc, (es, us, ws, vs, hs), x, n, ((1, nb - 1),))
        return carry

    lax.fori_loop(RIM, nx - RIM, rows, 0)

    def column(i, carry):
        x_column(field, u, acc, lax.rem(i, n), 1 + lax.div(i, n), ((RIM, nx - RIM),))
        return carry

    lax.fori_loop(0, n * (nb - 2), column, 0)


ANY = pl.BlockSpec(memory_space=pl.ANY)
INSIDE = pl.BlockSpec(memory_space=pltpu.VMEM)


def stream_scratch(nx, ny, nz):
    return [pltpu.VMEM((nz // LANES, ny + 3 * ROWS, LANES), jnp.float32)] * 5


def shapes(*dims):
    return jax.ShapeDtypeStruct(dims, jnp.float32)


def edge_rows(shape, field, acc, u, xa, xb, ya, yb):
    nx, ny, nz = shape
    return pl.pallas_call(
        edge_rows_kernel,
        in_specs=[INSIDE] * 3 + [ANY] * 4,
        out_specs=[INSIDE] * 2 + [ANY] * 2,
        out_shape=[rimmed(shape)] * 2 + [shapes(nx, RIM, nz)] * 2,
        input_output_aliases={0: 0, 1: 1},
        scratch_shapes=stream_scratch(nx, ny, nz)
        + [pltpu.VMEM((nx, RIM, nz), jnp.float32)] * 4
        + [pltpu.SemaphoreType.DMA((24,))],
        name="edge_rows",
        cost_estimate=estimate(shapes(*shape), 30),
        compiler_params=pltpu.CompilerParams(vmem_limit_bytes=8 * MIB),
    )(field, acc, u, xa, xb, ya, yb)


def edge_planes(shape, acc, field, u):
    nx, ny, nz = shape
    return pl.pallas_call(
        edge_planes_kernel,
        in_specs=[INSIDE] * 3,
        out_specs=[INSIDE] + [ANY] * 2,
        out_shape=[rimmed(shape)] + [shapes(RIM, ny + 2 * ROWS, nz)] * 2,
        input_output_aliases={0: 0},
        scratch_shapes=stream_scratch(nx, ny, nz) + [pltpu.SemaphoreType.DMA((8,))],
        name="edge_planes",
        cost_estimate=estimate(shapes(*shape), 20),
        compiler_params=pltpu.CompilerParams(vmem_limit_bytes=4 * MIB),
    )(acc, field, u)


def interior(shape, acc, field, u, after):
    nx, ny, nz = shape
    return pl.pallas_call(
        interior_kernel,
        in_specs=[INSIDE] * 3 + [ANY],
        out_specs=INSIDE,
        out_shape=rimmed(shape),
        input_output_aliases={0: 0},
        scratch_shapes=stream_scratch(nx, ny, nz),
        name="interior",
        cost_estimate=estimate(shapes(*shape), 60),
        compiler_params=pltpu.CompilerParams(vmem_limit_bytes=4 * MIB),
    )(acc, field, u, after)


def corner_kernel(ya_hbm, yb_hbm, bx_a, bx_b, out_a, out_b, rows, buffer, sem):
    nx, rim, nz = ya_hbm.shape
    copies = Copies(sem)
    faces, _ = face_starts(nx)
    upper = first_is_above("narrow")
    total = bx_a.shape[1]
    for i, face in enumerate(faces):
        copies.start(i, ya_hbm.at[pl.ds(face, RIM)], rows.at[2 * i])
        copies.start(i, yb_hbm.at[pl.ds(face, RIM)], rows.at[2 * i + 1])
    for i, out in enumerate((out_a, out_b)):
        copies.wait(i)
        for x in range(RIM):
            one, two = rows[2 * i, x], rows[2 * i + 1, x]
            buffer[2 * i, x, pl.ds(ROWS - RIM, RIM), :] = jnp.where(upper, two, one)
            buffer[2 * i + 1, x, pl.ds(0, RIM), :] = jnp.where(upper, one, two)
        copies.start("out", buffer.at[2 * i], out.at[:, pl.ds(0, ROWS), :])
        copies.start("out", buffer.at[2 * i + 1], out.at[:, pl.ds(total - ROWS, ROWS), :])
    copies.finish()


def with_corners(ya, yb, bx_a, bx_b):
    nx, rim, nz = ya.shape
    return pl.pallas_call(
        corner_kernel,
        in_specs=[ANY] * 4,
        out_specs=[ANY, ANY],
        out_shape=[shapes(*bx_a.shape)] * 2,
        input_output_aliases={2: 0, 3: 1},
        scratch_shapes=[
            pltpu.VMEM((4, RIM, RIM, nz), jnp.float32),
            pltpu.VMEM((4, RIM, ROWS, nz), jnp.float32),
            pltpu.SemaphoreType.DMA((8,)),
        ],
        name="with_corners",
        compiler_params=pltpu.CompilerParams(vmem_limit_bytes=4 * MIB),
    )(ya, yb, bx_a, bx_b)


def sweeps_kernel(f0_in, xa, xb, ya_hbm, yb_hbm, route_ref, perm_ref, zmean_ref, f0, out_hbm, *rest):
    slot_refs, (f1, step, sgn, ya, yb, sem) = rest[:-6], rest[-6:]
    nx, ny, nz = out_hbm.shape
    n = nz // LANES
    nb = ny // ROWS
    copies = Copies(sem)
    _, rims = face_starts(nx)
    upper = first_is_above("narrow")
    parts = pieces(nx)
    copies.start("rows", ya_hbm, ya)
    copies.start("rows", yb_hbm, yb)
    for block, rim in ((xa, rims[0]), (xb, rims[1])):
        for k, lanes in lane_chunks(nz):
            copies.start("rim", block.at[:, :, lanes], f0.at[pl.ds(rim, RIM), k])
    copies.wait("rows")
    place_rows(f0, RIM, nx, n, upper, ya, yb, ny)
    copies.wait("rim")

    def sweep(src, dst, x_first, x_end, y_first, blocks, mode):
        def plane(x, carry):
            for b in range(blocks):
                y = ROWS + y_first + b * ROWS
                ys = pl.ds(y, ROWS)
                f = [src[x, k, ys, :] for k in range(n)]
                fp = rolled(f, 1, lambda k: f[k])
                fm = rolled(f, -1, lambda k: f[k])
                for k in range(n):
                    if mode == "first":
                        st = (PSEUDO_STEP * f[k]) * lax.rsqrt(f[k] * f[k] + 1.0)
                        sg = jnp.where(f[k] > 0, 1.0, -1.0)
                        step[x, k, ys, :] = st
                        sgn[x, k, ys, :] = sg
                    else:
                        st = step[x, k, ys, :]
                        sg = sgn[x, k, ys, :]
                    p = sg * f[k]

                    def term(lo, hi):
                        m = jnp.maximum(p - jnp.minimum(sg * lo, sg * hi), 0.0)
                        return m * m

                    sq = term(src[x - 1, k, ys, :], src[x + 1, k, ys, :])
                    sq = sq + term(src[x, k, pl.ds(y - 1, ROWS), :], src[x, k, pl.ds(y + 1, ROWS), :])
                    sq = sq + term(fm[k], fp[k])
                    root = sq * lax.rsqrt(jnp.maximum(sq, 1e-30))
                    new = f[k] - st * (root - 1.0)
                    dst[x, k, ys, :] = new
                    if mode == "last":
                        sgn[x, k, ys, :] = new * lax.rsqrt(new * new + 1.0)
            return carry

        lax.fori_loop(x_first, x_end, plane, 0)

    sweep(f0, f1, 1, nx + 5, -2, nb + 1, "first")
    sweep(f1, f0, 2, nx + 4, -1, nb + 1, "middle")
    for x0, count in parts:
        sweep(f0, f1, RIM + x0, RIM + x0 + count, 0, nb, "last")
        for k, lanes in lane_chunks(nz):
            copies.start("out", f1.at[pl.ds(RIM + x0, count), k, pl.ds(ROWS, ny), :], out_hbm.at[pl.ds(x0, count), :, lanes])

    half = TILE // 2
    tz = nz // TILE
    blocks = [(tx, ty) for tx in range(nx // TILE) for ty in range(ny // TILE)]

    def two(a):
        high = a.astype(jnp.bfloat16)
        return high, (a - high.astype(jnp.float32)).astype(jnp.bfloat16)

    summed = []
    for tx, ty in blocks:
        for cx in range(half):
            row = []
            for k in range(n):
                x, y = RIM + tx * TILE + 2 * cx, ROWS + ty * TILE
                even, odd = pl.ds(y, half, 2), pl.ds(y + 1, half, 2)
                row.append((sgn[x, k, even, :] + sgn[x, k, odd, :]) + (sgn[x + 1, k, even, :] + sgn[x + 1, k, odd, :]))
            summed.append(jnp.concatenate(row, axis=1))
    summed = jnp.concatenate(summed, axis=0)
    zm = zmean_ref[...]
    dims = (((1,), (1,)), ((), ()))
    high, low = two(summed)
    mean = lax.dot_general(zm, high, dims, preferred_element_type=jnp.float32)
    mean = mean + lax.dot_general(zm, low, dims, preferred_element_type=jnp.float32)
    area = half * half
    tiles = jnp.concatenate(
        [
            jnp.concatenate([mean[c * tz : (c + 1) * tz, i * area : (i + 1) * area] for c in range(half)], axis=1)
            for i in range(len(blocks))
        ],
        axis=0,
    )
    pm = perm_ref[...]
    high, low = two(tiles)
    tiles = 0.5 - (jnp.dot(high, pm, preferred_element_type=jnp.float32) + jnp.dot(low, pm, preferred_element_type=jnp.float32))
    owners = len(slot_refs)
    capacity = slot_refs[0].shape[0]
    count = len(blocks) * tz
    route = route_ref[...] - lax.axis_index("wide")
    route = jnp.where(route < 0, route + owners, route)
    padded = -(-owners // ROWS) * ROWS
    matches = lax.broadcasted_iota(jnp.int32, (padded, count), 0) == route
    ordered = lax.broadcasted_iota(jnp.int32, (count, count), 0) < lax.broadcasted_iota(jnp.int32, (count, count), 1)
    match = jnp.where(matches, 1.0, 0.0)
    earlier = jnp.dot(
        match.astype(jnp.bfloat16), jnp.where(ordered, 1.0, 0.0).astype(jnp.bfloat16), preferred_element_type=jnp.float32
    )
    position = jnp.sum(earlier * match, axis=0, keepdims=True).astype(jnp.int32)
    target = route * capacity + position
    slots = lax.broadcasted_iota(jnp.int32, (owners * capacity, count), 0)
    pick = jnp.where(slots == target, 1.0, 0.0).astype(jnp.bfloat16)
    high, low = two(tiles)
    packed = jnp.dot(pick, high, preferred_element_type=jnp.float32) + jnp.dot(pick, low, preferred_element_type=jnp.float32)
    for i, ref in enumerate(slot_refs):
        ref[...] = packed[i * capacity : (i + 1) * capacity, :]
    copies.finish()


def sweeps(shape, moved, rims, route, owners, capacity):
    nx, ny, nz = shape
    n = nz // LANES
    f32 = jnp.float32
    half = TILE // 2
    tz = nz // TILE
    r = np.arange(half * tz)
    z = np.arange(nz)
    zmean = ((z[None, :] // TILE == (r % tz)[:, None]) & ((z[None, :] % TILE) // 2 == (r // tz)[:, None])) / 16.0
    src = np.arange(half**3)
    perm = np.zeros((half**3, half**3))
    perm[src, (src % half**2) * half + src // half**2] = 1.0
    return pl.pallas_call(
        sweeps_kernel,
        in_specs=[INSIDE] + [ANY] * 4 + [INSIDE] * 3,
        out_specs=[INSIDE, ANY] + [INSIDE] * owners,
        out_shape=[rimmed(shape), shapes(nx, ny, nz)] + [shapes(capacity, half**3)] * owners,
        input_output_aliases={0: 0},
        scratch_shapes=[rimmed(shape)] * 3 + [pltpu.VMEM((nx, RIM, nz), f32)] * 2 + [pltpu.SemaphoreType.DMA((64,))],
        name="sweeps",
        cost_estimate=estimate(shapes(*shape), 100),
        compiler_params=pltpu.CompilerParams(vmem_limit_bytes=30 * MIB),
    )(moved, *rims, route, jnp.asarray(perm, jnp.bfloat16), jnp.asarray(zmean, jnp.bfloat16))


def faces_kernel(core, xa_hbm, xb_hbm, ya_hbm, yb_hbm, x, rows, y, sem):
    nx, ny, nz = core.shape
    copies = Copies(sem)
    faces, _ = face_starts(nx)
    upper = first_is_above("narrow")
    groups = pieces(nx)
    copies.start("xa", core.at[pl.ds(faces[0], RIM)], x.at[0])
    copies.start("xb", core.at[pl.ds(faces[1], RIM)], x.at[1])
    for x0, count in groups:
        xs = pl.ds(x0, count)
        copies.start(x0, core.at[xs, pl.ds(0, ROWS), :], rows.at[0, xs])
        copies.start(x0, core.at[xs, pl.ds(ny - ROWS, ROWS), :], rows.at[1, xs])
    copies.wait("xa")
    copies.start("out", x.at[0], xa_hbm)
    copies.wait("xb")
    copies.start("out", x.at[1], xb_hbm)

    def plane(i, carry):
        lo, hi = rows[0, i, pl.ds(0, RIM), :], rows[1, i, pl.ds(ROWS - RIM, RIM), :]
        y[0, i] = jnp.where(upper, hi, lo)
        y[1, i] = jnp.where(upper, lo, hi)
        return carry

    for x0, count in groups:
        xs = pl.ds(x0, count)
        copies.wait(x0)
        lax.fori_loop(x0, x0 + count, plane, 0)
        copies.start("out", y.at[0, xs], ya_hbm.at[xs])
        copies.start("out", y.at[1, xs], yb_hbm.at[xs])
    copies.finish()


def own_faces(block):
    nx, ny, nz = block.shape
    f32 = jnp.float32
    return pl.pallas_call(
        faces_kernel,
        in_specs=[ANY],
        out_specs=[ANY] * 4,
        out_shape=[shapes(RIM, ny, nz)] * 2 + [shapes(nx, RIM, nz)] * 2,
        scratch_shapes=[
            pltpu.VMEM((2, RIM, ny, nz), f32),
            pltpu.VMEM((2, nx, ROWS, nz), f32),
            pltpu.VMEM((2, nx, RIM, nz), f32),
            pltpu.SemaphoreType.DMA((24,)),
        ],
        name="own_faces",
        compiler_params=pltpu.CompilerParams(vmem_limit_bytes=61 * MIB),
    )(block)


def gather_kernel(*refs):
    blocks, out, sem = refs[:-2], refs[-2], refs[-1]
    me, owners = lax.axis_index("wide"), len(blocks)
    copies = [
        pltpu.make_async_copy(b, out.at[lax.rem(me - i + owners, owners)], sem.at[i]) for i, b in enumerate(blocks)
    ]
    for c in copies:
        c.start()
    for c in copies:
        c.wait()


def gather_blocks(blocks):
    return pl.pallas_call(
        gather_kernel,
        in_specs=[INSIDE] * len(blocks),
        out_specs=ANY,
        out_shape=shapes(len(blocks), *blocks[0].shape),
        scratch_shapes=[pltpu.SemaphoreType.DMA((len(blocks),))],
        name="gather_blocks",
        compiler_params=pltpu.CompilerParams(vmem_limit_bytes=8 * MIB),
    )(*blocks)


def trade(axis, first, second):
    peers = lax.axis_size(axis)
    return (
        lax.ppermute(first, axis, [(i, i ^ 1) for i in range(peers)]),
        lax.ppermute(second, axis, [(i, (i + 1 if i % 2 else i - 1) % peers) for i in range(peers)]),
    )


def on_device(level_set, velocity, box_owner):
    owners = lax.axis_size("wide")
    xa, xb, ya, yb = own_faces(level_set)
    xa, xb = trade("wide", xa, xb)
    ya, yb = trade("narrow", ya, yb)
    field, acc, u = along_z(level_set, velocity)
    shape = level_set.shape
    field, acc, yf_a, yf_b = edge_rows(shape, field, acc, u, xa, xb, ya, yb)
    ya, yb = trade("narrow", yf_a, yf_b)
    acc, bx_a, bx_b = edge_planes(shape, acc, field, u)
    bx_a, bx_b = with_corners(ya, yb, bx_a, bx_b)
    xa, xb = trade("wide", bx_a, bx_b)
    moved = interior(shape, acc, field, u, bx_a)
    tile_count = box_owner.shape[2]
    capacity = max(2, 5 * tile_count // (2 * owners))
    route = box_owner.reshape(1, tile_count)
    _, surface, *slots = sweeps(shape, moved, (xa, xb, ya, yb), route, owners, capacity)
    received = [slots[0]]
    for step in range(1, owners):
        received.append(lax.ppermute(slots[step], "wide", [(i, (i + step) % owners) for i in range(owners)]))
    box_slots = gather_blocks(received)
    return (surface, box_slots.reshape(1, 1, owners * capacity, -1))


def solution(mesh):
    return jax.shard_map(
        on_device,
        mesh=mesh,
        in_specs=(
            P("wide", "narrow", None),
            P(None, "wide", "narrow", None),
            P("wide", "narrow", None, None),
        ),
        out_specs=(P("wide", "narrow", None), P("wide", "narrow", None, None)),
        check_vma=False,
    )
```

```python
import functools
import math
import jax
import jax.numpy as jnp
import numpy as np
from jax import lax
from jax.experimental import pallas as pl
from jax.experimental.pallas import tpu as pltpu
from jax.sharding import PartitionSpec as P

TILE = 16
WENO_EPS = 1e-06
PSEUDO_STEP = 0.3
RIM = 3
SECOND = 12
LANES = 128
ROWS = 8
MIB = 1024 * 1024


def correction(s1, s2, s3, h1, h0):
    r1 = 1.0 / s1
    r2 = 1.0 / s2
    r3 = 1.0 / s3
    w1 = (r1 * r1) * (1.0 / 3.0)
    w2 = (r2 * r2) * 2.0
    w3 = r3 * r3
    return (w1 * (4.0 * h1 - h0) + (w3 - w2) * h0) / ((w1 + w3) + w2)


def pair_forms(x, y, t):
    t2 = t + t
    q = t * t + 0.75 * WENO_EPS
    y75 = 0.75 * y
    w = q + y75 * x
    u = w + y75 * t2
    v = w - (0.75 * x) * t2
    return u, w, v


def rolled(chunks, shift, fill):
    lane = lax.broadcasted_iota(jnp.int32, chunks[0].shape, 1)
    turned = [pltpu.roll(c, (-shift) % LANES, 1) for c in chunks]
    out = []
    n = len(chunks)
    for k in range(n):
        other = k + (1 if shift > 0 else -1)
        beyond = turned[other] if 0 <= other < n else fill(k)
        mask = lane >= LANES - shift if shift > 0 else lane < -shift
        out.append(jnp.where(mask, beyond, turned[k]))
    return out


def along_z_kernel(core, u_hbm, field, acc, u, uz, sem):
    nx, ny, nz = core.shape
    copies = Copies(sem)
    bounds = [0, nx // 16, nx // 4, nx // 2, 3 * nx // 4, nx]
    groups = list(zip(bounds, bounds[1:]))
    for x0, x1 in groups:
        xs = pl.ds(x0, x1 - x0)
        for k, lanes in lane_chunks(nz):
            copies.start(x0, core.at[xs, :, lanes], field.at[pl.ds(x0 + RIM, x1 - x0), k, pl.ds(ROWS, ny), :])
        copies.start(x0, u_hbm.at[2, xs], uz.at[xs])
    copies.start("u", u_hbm.at[pl.ds(0, 2)], u)
    for x0, x1 in groups:
        copies.wait(x0)
        lax.fori_loop(x0, x1, functools.partial(z_plane, field, uz, acc, ny, nz), 0)
    copies.finish()


def z_plane(field, uz, acc, rows, depth, x, carry):
    n = depth // LANES
    zero = jnp.zeros((ROWS, LANES), jnp.float32)
    eps = 0.75 * WENO_EPS
    for yb in range(rows // ROWS):
        ys = pl.ds(yb * ROWS, ROWS)
        yf = pl.ds(yb * ROWS + ROWS, ROWS)
        f = [field[x + RIM, k, yf, :] for k in range(n)]
        fp = rolled(f, 1, lambda k: f[k])
        fm = rolled(f, -1, lambda k: f[k])
        e = [(fp[k] - f[k]) - (f[k] - fm[k]) for k in range(n)]
        ep = rolled(e, 1, lambda k: zero)
        em = rolled(e, -1, lambda k: zero)
        epp = rolled(e, 2, lambda k: zero)
        emm = rolled(e, -2, lambda k: zero)
        for k in range(n):
            v = uz[x, ys, pl.ds(k * LANES, LANES)].astype(jnp.float32)
            up = v > 0
            c = e[k]
            a = jnp.where(up, emm[k], epp[k])
            b = jnp.where(up, em[k], ep[k])
            d = jnp.where(up, ep[k], em[k])
            al, be, ga = b - a, c - b, d - c
            b75, c75 = 0.75 * b, 0.75 * c
            s1 = (al * al + eps) + b75 * (b + al)
            s2 = (be * be + eps) + b75 * c
            s3 = (ga * ga + eps) + c75 * (c - ga)
            phi = correction(s1, s2, s3, be - al, ga - be)
            mid = 6.0 * (fp[k] - fm[k]) - (ep[k] - em[k])
            v12 = v * (1.0 / 12.0)
            acc[x + RIM, k, yf, :] = f[k] - (v12 * mid - jnp.abs(v12) * phi)
    return carry


def in_vmem(shape, dtype=jnp.float32):
    return pltpu.VMEM(shape, dtype)


def rimmed(shape):
    nx, ny, nz = shape
    return in_vmem((nx + 2 * RIM, nz // LANES, ny + 2 * ROWS, LANES))


def along_z(level_set, velocity):
    nx, ny, nz = level_set.shape
    return pl.pallas_call(
        along_z_kernel,
        in_specs=[ANY, ANY],
        out_specs=[INSIDE] * 3,
        out_shape=[rimmed(level_set.shape)] * 2 + [in_vmem((2, nx, ny, nz), velocity.dtype)],
        scratch_shapes=[pltpu.VMEM((nx, ny, nz), velocity.dtype), pltpu.SemaphoreType.DMA((40,))],
        name="along_z",
        cost_estimate=estimate(level_set, 60),
        compiler_params=pltpu.CompilerParams(vmem_limit_bytes=46 * MIB),
    )(level_set, velocity)


def estimate(block, flops):
    return pl.CostEstimate(flops=flops * block.size, bytes_accessed=8 * block.size, transcendentals=4 * block.size)


class Copies:
    def __init__(self, sem):
        self.sem, self.used, self.groups = sem, 0, {}

    def start(self, group, src, dst):
        copy = pltpu.make_async_copy(src, dst, self.sem.at[self.used])
        self.used += 1
        copy.start()
        self.groups.setdefault(group, []).append(copy)

    def wait(self, group):
        for copy in self.groups.pop(group, ()):
            copy.wait()

    def finish(self):
        for group in list(self.groups):
            self.wait(group)


def lane_chunks(nz):
    return [(k, pl.ds(k * LANES, LANES)) for k in range(nz // LANES)]


def x_column(field, u, acc, k, yb, ranges):
    ys = pl.ds(pl.multiple_of(yb * ROWS, ROWS), ROWS)
    yf = pl.ds(pl.multiple_of(yb * ROWS + ROWS, ROWS), ROWS)
    lanes = pl.ds(pl.multiple_of(k * LANES, LANES), LANES)
    for first, last in ranges:
        f, g, e, t, h, pu, pw, pv = {}, {}, {}, {}, {}, {}, {}, {}

        def value(x):
            f[x] = field[x + RIM, k, yf, :]
            if x - 1 in f:
                g[x - 1] = f[x] - f[x - 1]
            if x - 2 in g:
                e[x - 1] = g[x - 1] - g[x - 2]
            if x - 2 in e:
                t[x - 2] = e[x - 1] - e[x - 2]
                pu[x - 2], pw[x - 2], pv[x - 2] = pair_forms(e[x - 2], e[x - 1], t[x - 2])
            if x - 3 in t:
                h[x - 2] = t[x - 2] - t[x - 3]

        for x in range(first - RIM, first + RIM):
            value(x)
        for x in range(first, last):
            value(x + RIM)
            v = u[0, x, ys, lanes].astype(jnp.float32)
            up = v > 0
            s1 = jnp.where(up, pu[x - 2], pv[x + 1])
            s2 = jnp.where(up, pw[x - 1], pw[x])
            s3 = jnp.where(up, pv[x], pu[x - 1])
            h1 = jnp.where(up, h[x - 1], h[x + 1])
            phi = correction(s1, s2, s3, h1, h[x])
            mid = 6.0 * (g[x] + g[x - 1]) - (e[x + 1] - e[x - 1])
            v12 = v * (1.0 / 12.0)
            acc[x + RIM, k, yf, :] = acc[x + RIM, k, yf, :] - (v12 * mid - jnp.abs(v12) * phi)


def y_plane(field, u, acc, streams, x, n, ranges):
    es, us, ws, vs, hs = streams
    for k in range(n):
        lanes = pl.ds(k * LANES, LANES)

        def at(y):
            return field[x + RIM, k, pl.ds(ROWS + y, ROWS), :]

        for first, last in ranges:
            for b in range(first, last + 1):
                y = b * ROWS - 2
                f0 = at(y)
                es[k, pl.ds(ROWS + b * ROWS, ROWS), :] = (at(y + 1) - f0) - (f0 - at(y - 1))
            for b in range(first, last + 1):
                r = ROWS + b * ROWS
                e0, e1, e_1 = es[k, pl.ds(r, ROWS), :], es[k, pl.ds(r + 1, ROWS), :], es[k, pl.ds(r - 1, ROWS), :]
                t = e1 - e0
                us[k, pl.ds(r, ROWS), :], ws[k, pl.ds(r, ROWS), :], vs[k, pl.ds(r, ROWS), :] = pair_forms(e0, e1, t)
                hs[k, pl.ds(r, ROWS), :] = t - (e0 - e_1)
            for b in range(first, last):
                ys, yf = pl.ds(b * ROWS, ROWS), pl.ds(b * ROWS + ROWS, ROWS)

                def of(ref, d):
                    return ref[k, pl.ds(ROWS + b * ROWS + 2 + d, ROWS), :]

                v = u[1, x, ys, lanes].astype(jnp.float32)
                up = v > 0
                s1 = jnp.where(up, of(us, -2), of(vs, 1))
                s2 = jnp.where(up, of(ws, -1), of(ws, 0))
                s3 = jnp.where(up, of(vs, 0), of(us, -1))
                h1 = jnp.where(up, of(hs, -1), of(hs, 1))
                phi = correction(s1, s2, s3, h1, of(hs, 0))
                mid = 6.0 * (at(b * ROWS + 1) - at(b * ROWS - 1)) - (of(es, 1) - of(es, -1))
                v12 = v * (1.0 / 12.0)
                acc[x + RIM, k, yf, :] = acc[x + RIM, k, yf, :] - (v12 * mid - jnp.abs(v12) * phi)


def place_rows(field, x0, count, upper, first, second, ny, second_at=0):
    n = field.shape[1]

    def body(i, carry):
        for k in range(n):
            one = first[k, pl.ds(RIM * i, RIM), :]
            two = second[k, pl.ds(second_at + RIM * i, RIM), :]
            field[i + x0, k, pl.ds(ROWS - RIM, RIM), :] = jnp.where(upper, two, one)
            field[i + x0, k, pl.ds(ROWS + ny, RIM), :] = jnp.where(upper, one, two)
        return carry

    lax.fori_loop(0, count, body, 0)


def side_shape(shape):
    nx, _, nz = shape
    return (nz // LANES, RIM * nx, LANES)


def first_is_above(axis):
    return lax.rem(lax.axis_index(axis), 2) == 0


def face_starts(nx):
    even = first_is_above("wide")
    faces = (jnp.where(even, nx - RIM, 0), jnp.where(even, 0, nx - RIM))
    rims = (jnp.where(even, nx + RIM, 0), jnp.where(even, 0, nx + RIM))
    return faces, rims


def pieces(nx):
    count = math.gcd(nx, 4)
    return [(i * (nx // count), nx // count) for i in range(count)]


def edge_rows_kernel(
    field_in, acc_in, u, xa, xb, ya_hbm, yb_hbm, field, acc, yfa_hbm, yfb_hbm, es, us, ws, vs, hs, ya, yb, yf_a, yf_b, sem
):
    _, nx, ny, nz = u.shape
    n, nb = nz // LANES, ny // ROWS
    copies = Copies(sem)
    streams = (es, us, ws, vs, hs)
    _, rims = face_starts(nx)
    upper = first_is_above("narrow")
    for block, rim in zip((xa, xb), rims):
        for k, lanes in lane_chunks(nz):
            copies.start("x", block.at[:, :, lanes], field.at[pl.ds(rim, RIM), k, pl.ds(ROWS, ny), :])
    copies.start("y", ya_hbm, ya)
    copies.start("y", yb_hbm, yb)
    copies.wait("x")

    def edge_column(i, carry):
        x_column(field, u, acc, lax.rem(i, n), lax.div(i, n) * (nb - 1), ((0, nx),))
        return carry

    lax.fori_loop(0, 2 * n, edge_column, 0)
    copies.wait("y")
    place_rows(field, RIM, nx, upper, ya, yb, ny)

    def edge_plane(x, carry):
        y_plane(field, u, acc, streams, x, n, ((0, 1), (nb - 1, nb)))
        for k in range(n):
            lo, hi = acc[x + RIM, k, pl.ds(ROWS, RIM), :], acc[x + RIM, k, pl.ds(ROWS + ny - RIM, RIM), :]
            yf_a[k, pl.ds(RIM * x, RIM), :] = jnp.where(upper, hi, lo)
            yf_b[k, pl.ds(RIM * x, RIM), :] = jnp.where(upper, lo, hi)
        return carry

    for x0, count in pieces(nx):
        rows = pl.ds(RIM * x0, RIM * count)
        lax.fori_loop(x0, x0 + count, edge_plane, 0)
        copies.start("out", yf_a.at[:, rows], yfa_hbm.at[:, rows])
        copies.start("out", yf_b.at[:, rows], yfb_hbm.at[:, rows])
    copies.finish()


def edge_planes_kernel(acc_in, field, u, acc, bx_a, bx_b, es, us, ws, vs, hs, sem):
    _, nx, ny, nz = u.shape
    n, nb = nz // LANES, ny // ROWS
    copies = Copies(sem)
    faces, _ = face_starts(nx)

    def both_ends(i, carry):
        y_plane(field, u, acc, (es, us, ws, vs, hs), jnp.where(i < RIM, i, nx - 2 * RIM + i), n, ((1, nb - 1),))
        return carry

    lax.fori_loop(0, 2 * RIM, both_ends, 0)

    def inner_column(i, carry):
        x_column(field, u, acc, lax.rem(i, n), 1 + lax.div(i, n), ((0, RIM), (nx - RIM, nx)))
        return carry

    lax.fori_loop(0, n * (nb - 2), inner_column, 0)
    rows = pl.ds(ROWS, ny)
    for face, out in zip(faces, (bx_a, bx_b)):
        for k, lanes in lane_chunks(nz):
            copies.start("out", acc.at[pl.ds(face + RIM, RIM), k, rows, :], out.at[:, :, lanes])
    copies.finish()


def interior_y_kernel(acc_in, field, u, after, acc, token, es, us, ws, vs, hs):
    _, nx, ny, nz = u.shape
    n, nb = nz // LANES, ny // ROWS

    def rows(x, carry):
        y_plane(field, u, acc, (es, us, ws, vs, hs), x, n, ((1, nb - 1),))
        return carry

    lax.fori_loop(RIM, nx - RIM, rows, 0)
    token[...] = jnp.zeros_like(token)


def interior_x_kernel(acc_in, field, u, acc):
    _, nx, ny, nz = u.shape
    n, nb = nz // LANES, ny // ROWS

    def column(i, carry):
        x_column(field, u, acc, lax.rem(i, n), 1 + lax.div(i, n), ((RIM, nx - RIM),))
        return carry

    lax.fori_loop(0, n * (nb - 2), column, 0)


ANY = pl.BlockSpec(memory_space=pl.ANY)
INSIDE = pl.BlockSpec(memory_space=pltpu.VMEM)


def stream_scratch(nx, ny, nz):
    return [pltpu.VMEM((nz // LANES, ny + 3 * ROWS, LANES), jnp.float32)] * 5


def shapes(*dims):
    return jax.ShapeDtypeStruct(dims, jnp.float32)


def edge_rows(shape, field, acc, u, xa, xb, ya, yb):
    nx, ny, nz = shape
    return pl.pallas_call(
        edge_rows_kernel,
        in_specs=[INSIDE] * 3 + [ANY] * 4,
        out_specs=[INSIDE] * 2 + [ANY] * 2,
        out_shape=[rimmed(shape)] * 2 + [shapes(*side_shape(shape))] * 2,
        input_output_aliases={0: 0, 1: 1},
        scratch_shapes=stream_scratch(nx, ny, nz)
        + [pltpu.VMEM(side_shape(shape), jnp.float32)] * 4
        + [pltpu.SemaphoreType.DMA((24,))],
        name="edge_rows",
        cost_estimate=estimate(shapes(*shape), 30),
        compiler_params=pltpu.CompilerParams(vmem_limit_bytes=8 * MIB),
    )(field, acc, u, xa, xb, ya, yb)


def edge_planes(shape, acc, field, u):
    nx, ny, nz = shape
    return pl.pallas_call(
        edge_planes_kernel,
        in_specs=[INSIDE] * 3,
        out_specs=[INSIDE] + [ANY] * 2,
        out_shape=[rimmed(shape)] + [shapes(RIM, ny, nz)] * 2,
        input_output_aliases={0: 0},
        scratch_shapes=stream_scratch(nx, ny, nz) + [pltpu.SemaphoreType.DMA((8,))],
        name="edge_planes",
        cost_estimate=estimate(shapes(*shape), 20),
        compiler_params=pltpu.CompilerParams(vmem_limit_bytes=4 * MIB),
    )(acc, field, u)


def interior_y(shape, acc, field, u, after):
    return pl.pallas_call(
        interior_y_kernel,
        in_specs=[INSIDE] * 3 + [ANY],
        out_specs=[INSIDE] * 2,
        out_shape=[rimmed(shape), shapes(ROWS, LANES)],
        input_output_aliases={0: 0},
        scratch_shapes=stream_scratch(*shape),
        name="interior_y",
        cost_estimate=estimate(shapes(*shape), 30),
        compiler_params=pltpu.CompilerParams(vmem_limit_bytes=4 * MIB),
    )(acc, field, u, after)


def interior_x(shape, acc, field, u):
    return pl.pallas_call(
        interior_x_kernel,
        in_specs=[INSIDE] * 3,
        out_specs=INSIDE,
        out_shape=rimmed(shape),
        input_output_aliases={0: 0},
        name="interior_x",
        cost_estimate=estimate(shapes(*shape), 30),
        compiler_params=pltpu.CompilerParams(vmem_limit_bytes=4 * MIB),
    )(acc, field, u)


def corner_kernel(ya, yb, token, ca, cb):
    n, rows, _ = ya.shape
    faces, _ = face_starts(rows // RIM)
    for k in range(n):
        for out, face in ((ca, faces[0]), (cb, faces[1])):
            for i in range(RIM):
                row = pl.ds(RIM * (face + i), RIM)
                out[k, pl.ds(RIM * i, RIM), :] = ya[k, row, :]
                out[k, pl.ds(SECOND + RIM * i, RIM), :] = yb[k, row, :]


def corner_faces(ya, yb, token):
    return pl.pallas_call(
        corner_kernel,
        in_specs=[INSIDE] * 3,
        out_specs=[INSIDE] * 2,
        out_shape=[shapes(ya.shape[0], 3 * ROWS, LANES)] * 2,
        name="corner_faces",
        compiler_params=pltpu.CompilerParams(vmem_limit_bytes=4 * MIB),
    )(ya, yb, token)


def sweeps_kernel(f0_in, xa, xb, ya, yb, ca, cb, route_ref, perm_ref, zmean_ref, f0, out_hbm, *rest):
    slot_refs, (f1, step, sgn, sem) = rest[:-4], rest[-4:]
    nx, ny, nz = out_hbm.shape
    n = nz // LANES
    nb = ny // ROWS
    copies = Copies(sem)
    _, rims = face_starts(nx)
    upper = first_is_above("narrow")
    parts = pieces(nx)
    for block, rim in ((xa, rims[0]), (xb, rims[1])):
        for k, lanes in lane_chunks(nz):
            copies.start("rim", block.at[:, :, lanes], f0.at[pl.ds(rim, RIM), k, pl.ds(ROWS, ny), :])
    place_rows(f0, RIM, nx, upper, ya, yb, ny)
    place_rows(f0, rims[0], RIM, upper, ca, ca, ny, SECOND)
    place_rows(f0, rims[1], RIM, upper, cb, cb, ny, SECOND)
    copies.wait("rim")

    def sweep(src, dst, x_first, x_end, y_first, blocks, mode):
        def plane(x, carry):
            for b in range(blocks):
                y = ROWS + y_first + b * ROWS
                ys = pl.ds(y, ROWS)
                f = [src[x, k, ys, :] for k in range(n)]
                fp = rolled(f, 1, lambda k: f[k])
                fm = rolled(f, -1, lambda k: f[k])
                for k in range(n):
                    if mode == "first":
                        st = (PSEUDO_STEP * f[k]) * lax.rsqrt(f[k] * f[k] + 1.0)
                        sg = jnp.where(f[k] > 0, 1.0, -1.0)
                        step[x, k, ys, :] = st
                        sgn[x, k, ys, :] = sg
                    else:
                        st = step[x, k, ys, :]
                        sg = sgn[x, k, ys, :]
                    p = sg * f[k]

                    def term(lo, hi):
                        m = jnp.maximum(p - jnp.minimum(sg * lo, sg * hi), 0.0)
                        return m * m

                    sq = term(src[x - 1, k, ys, :], src[x + 1, k, ys, :])
                    sq = sq + term(src[x, k, pl.ds(y - 1, ROWS), :], src[x, k, pl.ds(y + 1, ROWS), :])
                    sq = sq + term(fm[k], fp[k])
                    root = sq * lax.rsqrt(jnp.maximum(sq, 1e-30))
                    new = f[k] - st * (root - 1.0)
                    dst[x, k, ys, :] = new
                    if mode == "last":
                        sgn[x, k, ys, :] = new * lax.rsqrt(new * new + 1.0)
            return carry

        lax.fori_loop(x_first, x_end, plane, 0)

    sweep(f0, f1, 1, nx + 5, -2, nb + 1, "first")
    sweep(f1, f0, 2, nx + 4, -1, nb + 1, "middle")
    for x0, count in parts:
        sweep(f0, f1, RIM + x0, RIM + x0 + count, 0, nb, "last")
        for k, lanes in lane_chunks(nz):
            copies.start("out", f1.at[pl.ds(RIM + x0, count), k, pl.ds(ROWS, ny), :], out_hbm.at[pl.ds(x0, count), :, lanes])

    half = TILE // 2
    tz = nz // TILE
    blocks = [(tx, ty) for tx in range(nx // TILE) for ty in range(ny // TILE)]

    def two(a):
        high = a.astype(jnp.bfloat16)
        return high, (a - high.astype(jnp.float32)).astype(jnp.bfloat16)

    summed = []
    for tx, ty in blocks:
        for cx in range(half):
            row = []
            for k in range(n):
                x, y = RIM + tx * TILE + 2 * cx, ROWS + ty * TILE
                even, odd = pl.ds(y, half, 2), pl.ds(y + 1, half, 2)
                row.append((sgn[x, k, even, :] + sgn[x, k, odd, :]) + (sgn[x + 1, k, even, :] + sgn[x + 1, k, odd, :]))
            summed.append(jnp.concatenate(row, axis=1))
    summed = jnp.concatenate(summed, axis=0)
    zm = zmean_ref[...]
    dims = (((1,), (1,)), ((), ()))
    high, low = two(summed)
    mean = lax.dot_general(zm, high, dims, preferred_element_type=jnp.float32)
    mean = mean + lax.dot_general(zm, low, dims, preferred_element_type=jnp.float32)
    area = half * half
    tiles = jnp.concatenate(
        [
            jnp.concatenate([mean[c * tz : (c + 1) * tz, i * area : (i + 1) * area] for c in range(half)], axis=1)
            for i in range(len(blocks))
        ],
        axis=0,
    )
    pm = perm_ref[...]
    high, low = two(tiles)
    tiles = 0.5 - (jnp.dot(high, pm, preferred_element_type=jnp.float32) + jnp.dot(low, pm, preferred_element_type=jnp.float32))
    owners = len(slot_refs)
    capacity = slot_refs[0].shape[0]
    count = len(blocks) * tz
    route = route_ref[...] - lax.axis_index("wide")
    route = jnp.where(route < 0, route + owners, route)
    padded = -(-owners // ROWS) * ROWS
    matches = lax.broadcasted_iota(jnp.int32, (padded, count), 0) == route
    ordered = lax.broadcasted_iota(jnp.int32, (count, count), 0) < lax.broadcasted_iota(jnp.int32, (count, count), 1)
    match = jnp.where(matches, 1.0, 0.0)
    earlier = jnp.dot(
        match.astype(jnp.bfloat16), jnp.where(ordered, 1.0, 0.0).astype(jnp.bfloat16), preferred_element_type=jnp.float32
    )
    position = jnp.sum(earlier * match, axis=0, keepdims=True).astype(jnp.int32)
    target = route * capacity + position
    slots = lax.broadcasted_iota(jnp.int32, (owners * capacity, count), 0)
    pick = jnp.where(slots == target, 1.0, 0.0).astype(jnp.bfloat16)
    high, low = two(tiles)
    packed = jnp.dot(pick, high, preferred_element_type=jnp.float32) + jnp.dot(pick, low, preferred_element_type=jnp.float32)
    for i, ref in enumerate(slot_refs):
        ref[...] = packed[i * capacity : (i + 1) * capacity, :]
    copies.finish()


def sweeps(shape, moved, rims, route, owners, capacity):
    nx, ny, nz = shape
    half = TILE // 2
    tz = nz // TILE
    r = np.arange(half * tz)
    z = np.arange(nz)
    zmean = ((z[None, :] // TILE == (r % tz)[:, None]) & ((z[None, :] % TILE) // 2 == (r // tz)[:, None])) / 16.0
    src = np.arange(half**3)
    perm = np.zeros((half**3, half**3))
    perm[src, (src % half**2) * half + src // half**2] = 1.0
    return pl.pallas_call(
        sweeps_kernel,
        in_specs=[INSIDE] + [ANY] * 2 + [INSIDE] * 7,
        out_specs=[INSIDE, ANY] + [INSIDE] * owners,
        out_shape=[rimmed(shape), shapes(nx, ny, nz)] + [shapes(capacity, half**3)] * owners,
        input_output_aliases={0: 0},
        scratch_shapes=[rimmed(shape)] * 3 + [pltpu.SemaphoreType.DMA((64,))],
        name="sweeps",
        cost_estimate=estimate(shapes(*shape), 100),
        compiler_params=pltpu.CompilerParams(vmem_limit_bytes=30 * MIB),
    )(moved, *rims, route, jnp.asarray(perm, jnp.bfloat16), jnp.asarray(zmean, jnp.bfloat16))


def faces_kernel(core, xa_hbm, xb_hbm, ya_hbm, yb_hbm, x, rows, y, sem):
    nx, ny, nz = core.shape
    copies = Copies(sem)
    faces, _ = face_starts(nx)
    upper = first_is_above("narrow")
    groups = pieces(nx)
    copies.start("xa", core.at[pl.ds(faces[0], RIM)], x.at[0])
    copies.start("xb", core.at[pl.ds(faces[1], RIM)], x.at[1])
    for x0, count in groups:
        xs = pl.ds(x0, count)
        copies.start(x0, core.at[xs, pl.ds(0, ROWS), :], rows.at[0, xs])
        copies.start(x0, core.at[xs, pl.ds(ny - ROWS, ROWS), :], rows.at[1, xs])
    copies.wait("xa")
    copies.start("out", x.at[0], xa_hbm)
    copies.wait("xb")
    copies.start("out", x.at[1], xb_hbm)

    def plane(i, carry):
        for k, lanes in lane_chunks(nz):
            lo, hi = rows[0, i, pl.ds(0, RIM), lanes], rows[1, i, pl.ds(ROWS - RIM, RIM), lanes]
            y[0, k, pl.ds(RIM * i, RIM), :] = jnp.where(upper, hi, lo)
            y[1, k, pl.ds(RIM * i, RIM), :] = jnp.where(upper, lo, hi)
        return carry

    for x0, count in groups:
        side = pl.ds(RIM * x0, RIM * count)
        copies.wait(x0)
        lax.fori_loop(x0, x0 + count, plane, 0)
        copies.start("out", y.at[0, :, side], ya_hbm.at[:, side])
        copies.start("out", y.at[1, :, side], yb_hbm.at[:, side])
    copies.finish()


def own_faces(block):
    nx, ny, nz = block.shape
    f32 = jnp.float32
    return pl.pallas_call(
        faces_kernel,
        in_specs=[ANY],
        out_specs=[ANY] * 4,
        out_shape=[shapes(RIM, ny, nz)] * 2 + [shapes(*side_shape(block.shape))] * 2,
        scratch_shapes=[
            pltpu.VMEM((2, RIM, ny, nz), f32),
            pltpu.VMEM((2, nx, ROWS, nz), f32),
            pltpu.VMEM((2,) + side_shape(block.shape), f32),
            pltpu.SemaphoreType.DMA((24,)),
        ],
        name="own_faces",
        compiler_params=pltpu.CompilerParams(vmem_limit_bytes=61 * MIB),
    )(block)


def gather_kernel(*refs):
    blocks, out, sem = refs[:-2], refs[-2], refs[-1]
    me, owners = lax.axis_index("wide"), len(blocks)
    copies = [
        pltpu.make_async_copy(b, out.at[lax.rem(me - i + owners, owners)], sem.at[i]) for i, b in enumerate(blocks)
    ]
    for c in copies:
        c.start()
    for c in copies:
        c.wait()


def gather_blocks(blocks):
    return pl.pallas_call(
        gather_kernel,
        in_specs=[INSIDE] * len(blocks),
        out_specs=ANY,
        out_shape=shapes(len(blocks), *blocks[0].shape),
        scratch_shapes=[pltpu.SemaphoreType.DMA((len(blocks),))],
        name="gather_blocks",
        compiler_params=pltpu.CompilerParams(vmem_limit_bytes=8 * MIB),
    )(*blocks)


def trade(axis, first, second):
    peers = lax.axis_size(axis)
    return (
        lax.ppermute(first, axis, [(i, i ^ 1) for i in range(peers)]),
        lax.ppermute(second, axis, [(i, (i + 1 if i % 2 else i - 1) % peers) for i in range(peers)]),
    )


def on_device(level_set, velocity, box_owner):
    owners = lax.axis_size("wide")
    xa, xb, ya, yb = own_faces(level_set)
    xa, xb = trade("wide", xa, xb)
    ya, yb = trade("narrow", ya, yb)
    field, acc, u = along_z(level_set, velocity)
    shape = level_set.shape
    field, acc, yf_a, yf_b = edge_rows(shape, field, acc, u, xa, xb, ya, yb)
    ya, yb = trade("narrow", yf_a, yf_b)
    acc, bx_a, bx_b = edge_planes(shape, acc, field, u)
    xa, xb = trade("wide", bx_a, bx_b)
    acc, token = interior_y(shape, acc, field, u, bx_a)
    ca, cb = trade("wide", *corner_faces(ya, yb, token))
    moved = interior_x(shape, acc, field, u)
    tile_count = box_owner.shape[2]
    capacity = max(2, 5 * tile_count // (2 * owners))
    route = box_owner.reshape(1, tile_count)
    _, surface, *slots = sweeps(shape, moved, (xa, xb, ya, yb, ca, cb), route, owners, capacity)
    received = [slots[0]]
    for step in range(1, owners):
        received.append(lax.ppermute(slots[step], "wide", [(i, (i + step) % owners) for i in range(owners)]))
    box_slots = gather_blocks(received)
    return (surface, box_slots.reshape(1, 1, owners * capacity, -1))


def solution(mesh):
    return jax.shard_map(
        on_device,
        mesh=mesh,
        in_specs=(
            P("wide", "narrow", None),
            P(None, "wide", "narrow", None),
            P("wide", "narrow", None, None),
        ),
        out_specs=(P("wide", "narrow", None), P("wide", "narrow", None, None)),
        check_vma=False,
    )
```

```python
import functools
import math
import jax
import jax.numpy as jnp
import numpy as np
from jax import lax
from jax.experimental import pallas as pl
from jax.experimental.pallas import tpu as pltpu
from jax.sharding import PartitionSpec as P

TILE = 16
WENO_EPS = 1e-06
PSEUDO_STEP = 0.3
RIM = 3
SECOND = 12
LANES = 128
ROWS = 8
MIB = 1024 * 1024


def correction(s1, s2, s3, h1, h0):
    r1 = 1.0 / s1
    r2 = 1.0 / s2
    r3 = 1.0 / s3
    w1 = (r1 * r1) * (1.0 / 3.0)
    w2 = (r2 * r2) * 2.0
    w3 = r3 * r3
    return (w1 * (4.0 * h1 - h0) + (w3 - w2) * h0) / ((w1 + w3) + w2)


def pair_forms(x, y, t):
    t2 = t + t
    q = t * t + 0.75 * WENO_EPS
    y75 = 0.75 * y
    w = q + y75 * x
    u = w + y75 * t2
    v = w - (0.75 * x) * t2
    return u, w, v


def rolled(chunks, shift, fill):
    lane = lax.broadcasted_iota(jnp.int32, chunks[0].shape, 1)
    turned = [pltpu.roll(c, (-shift) % LANES, 1) for c in chunks]
    out = []
    n = len(chunks)
    for k in range(n):
        other = k + (1 if shift > 0 else -1)
        beyond = turned[other] if 0 <= other < n else fill(k)
        mask = lane >= LANES - shift if shift > 0 else lane < -shift
        out.append(jnp.where(mask, beyond, turned[k]))
    return out


def along_z_kernel(core, u_hbm, field, acc, u, uz, ft, ut, es, us, ws, vs, hs, sem):
    nx, ny, nz = core.shape
    copies = Copies(sem)
    bounds = [0, nx // 16, nx // 4, nx // 2, 3 * nx // 4, nx]
    groups = list(zip(bounds, bounds[1:]))
    for x0, x1 in groups:
        xs = pl.ds(x0, x1 - x0)
        for k, lanes in lane_chunks(nz):
            copies.start(x0, core.at[xs, :, lanes], field.at[pl.ds(x0 + RIM, x1 - x0), k, pl.ds(ROWS, ny), :])
        copies.start(x0, u_hbm.at[2, xs], uz.at[xs])
    copies.start("u", u_hbm.at[pl.ds(0, 2)], u)
    per = LANES // ny
    for x0, x1 in groups:
        copies.wait(x0)
        lax.fori_loop(x0 // per, x1 // per, functools.partial(z_planes, field, uz, acc, ft, ut, (es, us, ws, vs, hs), per), 0)
    copies.finish()


def z_planes(field, uz, acc, ft, ut, streams, per, i, carry):
    es, us, ws, vs, hs = streams
    ny = LANES // per
    n = field.shape[1]
    depth = n * LANES
    rows = pl.ds(ROWS, ny)
    planes = [per * i + p for p in range(per)]
    for k in range(n):
        ft[pl.ds(ROWS + k * LANES, LANES), :] = jnp.concatenate([field[x + RIM, k, rows, :] for x in planes], axis=0).T
        v = jnp.concatenate([uz[x, :, pl.ds(k * LANES, LANES)] for x in planes], axis=0)
        ut[pl.ds(k * LANES, LANES), :] = v.astype(jnp.float32).T
    ft[pl.ds(0, ROWS), :] = jnp.broadcast_to(ft[pl.ds(ROWS, 1), :], (ROWS, LANES))
    ft[pl.ds(ROWS + depth, ROWS), :] = jnp.broadcast_to(ft[pl.ds(ROWS + depth - 1, 1), :], (ROWS, LANES))

    def at(z):
        return ft[pl.ds(ROWS + z, ROWS), :]

    blocks = depth // ROWS
    for b in range(blocks + 1):
        z = b * ROWS - 2
        f0 = at(z)
        es[pl.ds(ROWS + b * ROWS, ROWS), :] = (at(z + 1) - f0) - (f0 - at(z - 1))
    for b in range(blocks + 1):
        r = ROWS + b * ROWS
        e0, e1, e_1 = es[pl.ds(r, ROWS), :], es[pl.ds(r + 1, ROWS), :], es[pl.ds(r - 1, ROWS), :]
        t = e1 - e0
        us[pl.ds(r, ROWS), :], ws[pl.ds(r, ROWS), :], vs[pl.ds(r, ROWS), :] = pair_forms(e0, e1, t)
        hs[pl.ds(r, ROWS), :] = t - (e0 - e_1)
    for b in range(blocks):

        def of(ref, d):
            return ref[pl.ds(ROWS + b * ROWS + 2 + d, ROWS), :]

        zs = pl.ds(b * ROWS, ROWS)
        v = ut[zs, :]
        up = v > 0
        s1 = jnp.where(up, of(us, -2), of(vs, 1))
        s2 = jnp.where(up, of(ws, -1), of(ws, 0))
        s3 = jnp.where(up, of(vs, 0), of(us, -1))
        h1 = jnp.where(up, of(hs, -1), of(hs, 1))
        phi = correction(s1, s2, s3, h1, of(hs, 0))
        mid = 6.0 * (at(b * ROWS + 1) - at(b * ROWS - 1)) - (of(es, 1) - of(es, -1))
        v12 = v * (1.0 / 12.0)
        ut[zs, :] = v12 * mid - jnp.abs(v12) * phi
    for k in range(n):
        change = ut[pl.ds(k * LANES, LANES), :].T
        for p, x in enumerate(planes):
            acc[x + RIM, k, rows, :] = field[x + RIM, k, rows, :] - change[p * ny : (p + 1) * ny, :]
    return carry


def in_vmem(shape, dtype=jnp.float32):
    return pltpu.VMEM(shape, dtype)


def rimmed(shape):
    nx, ny, nz = shape
    return in_vmem((nx + 2 * RIM, nz // LANES, ny + 2 * ROWS, LANES))


def along_z(level_set, velocity):
    nx, ny, nz = level_set.shape
    return pl.pallas_call(
        along_z_kernel,
        in_specs=[ANY, ANY],
        out_specs=[INSIDE] * 3,
        out_shape=[rimmed(level_set.shape)] * 2 + [in_vmem((2, nx, ny, nz), velocity.dtype)],
        scratch_shapes=[
            pltpu.VMEM((nx, ny, nz), velocity.dtype),
            pltpu.VMEM((nz + 2 * ROWS, LANES), jnp.float32),
            pltpu.VMEM((nz, LANES), jnp.float32),
        ]
        + [pltpu.VMEM((nz + 3 * ROWS, LANES), jnp.float32)] * 5
        + [pltpu.SemaphoreType.DMA((40,))],
        name="along_z",
        cost_estimate=estimate(level_set, 60),
        compiler_params=pltpu.CompilerParams(vmem_limit_bytes=46 * MIB),
    )(level_set, velocity)


def estimate(block, flops):
    return pl.CostEstimate(flops=flops * block.size, bytes_accessed=8 * block.size, transcendentals=4 * block.size)


class Copies:
    def __init__(self, sem):
        self.sem, self.used, self.groups = sem, 0, {}

    def start(self, group, src, dst):
        copy = pltpu.make_async_copy(src, dst, self.sem.at[self.used])
        self.used += 1
        copy.start()
        self.groups.setdefault(group, []).append(copy)

    def wait(self, group):
        for copy in self.groups.pop(group, ()):
            copy.wait()

    def finish(self):
        for group in list(self.groups):
            self.wait(group)


def lane_chunks(nz):
    return [(k, pl.ds(k * LANES, LANES)) for k in range(nz // LANES)]


def x_column(field, u, acc, k, yb, ranges):
    ys = pl.ds(pl.multiple_of(yb * ROWS, ROWS), ROWS)
    yf = pl.ds(pl.multiple_of(yb * ROWS + ROWS, ROWS), ROWS)
    lanes = pl.ds(pl.multiple_of(k * LANES, LANES), LANES)
    for first, last in ranges:
        f, g, e, t, h, pu, pw, pv = {}, {}, {}, {}, {}, {}, {}, {}

        def value(x):
            f[x] = field[x + RIM, k, yf, :]
            if x - 1 in f:
                g[x - 1] = f[x] - f[x - 1]
            if x - 2 in g:
                e[x - 1] = g[x - 1] - g[x - 2]
            if x - 2 in e:
                t[x - 2] = e[x - 1] - e[x - 2]
                pu[x - 2], pw[x - 2], pv[x - 2] = pair_forms(e[x - 2], e[x - 1], t[x - 2])
            if x - 3 in t:
                h[x - 2] = t[x - 2] - t[x - 3]

        for x in range(first - RIM, first + RIM):
            value(x)
        for x in range(first, last):
            value(x + RIM)
            v = u[0, x, ys, lanes].astype(jnp.float32)
            up = v > 0
            s1 = jnp.where(up, pu[x - 2], pv[x + 1])
            s2 = jnp.where(up, pw[x - 1], pw[x])
            s3 = jnp.where(up, pv[x], pu[x - 1])
            h1 = jnp.where(up, h[x - 1], h[x + 1])
            phi = correction(s1, s2, s3, h1, h[x])
            mid = 6.0 * (g[x] + g[x - 1]) - (e[x + 1] - e[x - 1])
            v12 = v * (1.0 / 12.0)
            acc[x + RIM, k, yf, :] = acc[x + RIM, k, yf, :] - (v12 * mid - jnp.abs(v12) * phi)


def y_plane(field, u, acc, streams, x, n, ranges):
    es, us, ws, vs, hs = streams
    for k in range(n):
        lanes = pl.ds(k * LANES, LANES)

        def at(y):
            return field[x + RIM, k, pl.ds(ROWS + y, ROWS), :]

        for first, last in ranges:
            for b in range(first, last + 1):
                y = b * ROWS - 2
                f0 = at(y)
                es[k, pl.ds(ROWS + b * ROWS, ROWS), :] = (at(y + 1) - f0) - (f0 - at(y - 1))
            for b in range(first, last + 1):
                r = ROWS + b * ROWS
                e0, e1, e_1 = es[k, pl.ds(r, ROWS), :], es[k, pl.ds(r + 1, ROWS), :], es[k, pl.ds(r - 1, ROWS), :]
                t = e1 - e0
                us[k, pl.ds(r, ROWS), :], ws[k, pl.ds(r, ROWS), :], vs[k, pl.ds(r, ROWS), :] = pair_forms(e0, e1, t)
                hs[k, pl.ds(r, ROWS), :] = t - (e0 - e_1)
            for b in range(first, last):
                ys, yf = pl.ds(b * ROWS, ROWS), pl.ds(b * ROWS + ROWS, ROWS)

                def of(ref, d):
                    return ref[k, pl.ds(ROWS + b * ROWS + 2 + d, ROWS), :]

                v = u[1, x, ys, lanes].astype(jnp.float32)
                up = v > 0
                s1 = jnp.where(up, of(us, -2), of(vs, 1))
                s2 = jnp.where(up, of(ws, -1), of(ws, 0))
                s3 = jnp.where(up, of(vs, 0), of(us, -1))
                h1 = jnp.where(up, of(hs, -1), of(hs, 1))
                phi = correction(s1, s2, s3, h1, of(hs, 0))
                mid = 6.0 * (at(b * ROWS + 1) - at(b * ROWS - 1)) - (of(es, 1) - of(es, -1))
                v12 = v * (1.0 / 12.0)
                acc[x + RIM, k, yf, :] = acc[x + RIM, k, yf, :] - (v12 * mid - jnp.abs(v12) * phi)


def place_rows(field, x0, count, upper, first, second, ny, second_at=0):
    n = field.shape[1]

    def body(i, carry):
        for k in range(n):
            one = first[k, pl.ds(RIM * i, RIM), :]
            two = second[k, pl.ds(second_at + RIM * i, RIM), :]
            field[i + x0, k, pl.ds(ROWS - RIM, RIM), :] = jnp.where(upper, two, one)
            field[i + x0, k, pl.ds(ROWS + ny, RIM), :] = jnp.where(upper, one, two)
        return carry

    lax.fori_loop(0, count, body, 0)


def side_shape(shape):
    nx, _, nz = shape
    return (nz // LANES, RIM * nx, LANES)


def first_is_above(axis):
    return lax.rem(lax.axis_index(axis), 2) == 0


def face_starts(nx):
    even = first_is_above("wide")
    faces = (jnp.where(even, nx - RIM, 0), jnp.where(even, 0, nx - RIM))
    rims = (jnp.where(even, nx + RIM, 0), jnp.where(even, 0, nx + RIM))
    return faces, rims


def pieces(nx):
    count = math.gcd(nx, 4)
    return [(i * (nx // count), nx // count) for i in range(count)]


def edge_rows_kernel(
    field_in, acc_in, u, xa, xb, ya_hbm, yb_hbm, field, acc, yfa_hbm, yfb_hbm, es, us, ws, vs, hs, ya, yb, yf_a, yf_b, sem
):
    _, nx, ny, nz = u.shape
    n, nb = nz // LANES, ny // ROWS
    copies = Copies(sem)
    streams = (es, us, ws, vs, hs)
    _, rims = face_starts(nx)
    upper = first_is_above("narrow")
    for block, rim in zip((xa, xb), rims):
        for k, lanes in lane_chunks(nz):
            copies.start("x", block.at[:, :, lanes], field.at[pl.ds(rim, RIM), k, pl.ds(ROWS, ny), :])
    copies.start("y", ya_hbm, ya)
    copies.start("y", yb_hbm, yb)
    copies.wait("x")

    def edge_column(i, carry):
        x_column(field, u, acc, lax.rem(i, n), lax.div(i, n) * (nb - 1), ((0, nx),))
        return carry

    lax.fori_loop(0, 2 * n, edge_column, 0)
    copies.wait("y")
    place_rows(field, RIM, nx, upper, ya, yb, ny)

    def edge_plane(x, carry):
        y_plane(field, u, acc, streams, x, n, ((0, 1), (nb - 1, nb)))
        for k in range(n):
            lo, hi = acc[x + RIM, k, pl.ds(ROWS, RIM), :], acc[x + RIM, k, pl.ds(ROWS + ny - RIM, RIM), :]
            yf_a[k, pl.ds(RIM * x, RIM), :] = jnp.where(upper, hi, lo)
            yf_b[k, pl.ds(RIM * x, RIM), :] = jnp.where(upper, lo, hi)
        return carry

    for x0, count in pieces(nx):
        rows = pl.ds(RIM * x0, RIM * count)
        lax.fori_loop(x0, x0 + count, edge_plane, 0)
        copies.start("out", yf_a.at[:, rows], yfa_hbm.at[:, rows])
        copies.start("out", yf_b.at[:, rows], yfb_hbm.at[:, rows])
    copies.finish()


def edge_planes_kernel(acc_in, field, u, acc, bx_a, bx_b, es, us, ws, vs, hs, sem):
    _, nx, ny, nz = u.shape
    n, nb = nz // LANES, ny // ROWS
    copies = Copies(sem)
    faces, _ = face_starts(nx)

    def both_ends(i, carry):
        y_plane(field, u, acc, (es, us, ws, vs, hs), jnp.where(i < RIM, i, nx - 2 * RIM + i), n, ((1, nb - 1),))
        return carry

    lax.fori_loop(0, 2 * RIM, both_ends, 0)

    def inner_column(i, carry):
        x_column(field, u, acc, lax.rem(i, n), 1 + lax.div(i, n), ((0, RIM), (nx - RIM, nx)))
        return carry

    lax.fori_loop(0, n * (nb - 2), inner_column, 0)
    rows = pl.ds(ROWS, ny)
    for face, out in zip(faces, (bx_a, bx_b)):
        for k, lanes in lane_chunks(nz):
            copies.start("out", acc.at[pl.ds(face + RIM, RIM), k, rows, :], out.at[:, :, lanes])
    copies.finish()


def interior_y_kernel(acc_in, field, u, after, acc, token, es, us, ws, vs, hs):
    _, nx, ny, nz = u.shape
    n, nb = nz // LANES, ny // ROWS

    def rows(x, carry):
        y_plane(field, u, acc, (es, us, ws, vs, hs), x, n, ((1, nb - 1),))
        return carry

    lax.fori_loop(RIM, nx - RIM, rows, 0)
    token[...] = jnp.zeros_like(token)


def interior_x_kernel(acc_in, field, u, acc):
    _, nx, ny, nz = u.shape
    n, nb = nz // LANES, ny // ROWS

    def column(i, carry):
        x_column(field, u, acc, lax.rem(i, n), 1 + lax.div(i, n), ((RIM, nx - RIM),))
        return carry

    lax.fori_loop(0, n * (nb - 2), column, 0)


ANY = pl.BlockSpec(memory_space=pl.ANY)
INSIDE = pl.BlockSpec(memory_space=pltpu.VMEM)


def stream_scratch(nx, ny, nz):
    return [pltpu.VMEM((nz // LANES, ny + 3 * ROWS, LANES), jnp.float32)] * 5


def shapes(*dims):
    return jax.ShapeDtypeStruct(dims, jnp.float32)


def edge_rows(shape, field, acc, u, xa, xb, ya, yb):
    nx, ny, nz = shape
    return pl.pallas_call(
        edge_rows_kernel,
        in_specs=[INSIDE] * 3 + [ANY] * 4,
        out_specs=[INSIDE] * 2 + [ANY] * 2,
        out_shape=[rimmed(shape)] * 2 + [shapes(*side_shape(shape))] * 2,
        input_output_aliases={0: 0, 1: 1},
        scratch_shapes=stream_scratch(nx, ny, nz)
        + [pltpu.VMEM(side_shape(shape), jnp.float32)] * 4
        + [pltpu.SemaphoreType.DMA((24,))],
        name="edge_rows",
        cost_estimate=estimate(shapes(*shape), 30),
        compiler_params=pltpu.CompilerParams(vmem_limit_bytes=8 * MIB),
    )(field, acc, u, xa, xb, ya, yb)


def edge_planes(shape, acc, field, u):
    nx, ny, nz = shape
    return pl.pallas_call(
        edge_planes_kernel,
        in_specs=[INSIDE] * 3,
        out_specs=[INSIDE] + [ANY] * 2,
        out_shape=[rimmed(shape)] + [shapes(RIM, ny, nz)] * 2,
        input_output_aliases={0: 0},
        scratch_shapes=stream_scratch(nx, ny, nz) + [pltpu.SemaphoreType.DMA((8,))],
        name="edge_planes",
        cost_estimate=estimate(shapes(*shape), 20),
        compiler_params=pltpu.CompilerParams(vmem_limit_bytes=4 * MIB),
    )(acc, field, u)


def interior_y(shape, acc, field, u, after):
    return pl.pallas_call(
        interior_y_kernel,
        in_specs=[INSIDE] * 3 + [ANY],
        out_specs=[INSIDE] * 2,
        out_shape=[rimmed(shape), shapes(ROWS, LANES)],
        input_output_aliases={0: 0},
        scratch_shapes=stream_scratch(*shape),
        name="interior_y",
        cost_estimate=estimate(shapes(*shape), 30),
        compiler_params=pltpu.CompilerParams(vmem_limit_bytes=4 * MIB),
    )(acc, field, u, after)


def interior_x(shape, acc, field, u):
    return pl.pallas_call(
        interior_x_kernel,
        in_specs=[INSIDE] * 3,
        out_specs=INSIDE,
        out_shape=rimmed(shape),
        input_output_aliases={0: 0},
        name="interior_x",
        cost_estimate=estimate(shapes(*shape), 30),
        compiler_params=pltpu.CompilerParams(vmem_limit_bytes=4 * MIB),
    )(acc, field, u)


def corner_kernel(ya, yb, token, ca, cb):
    n, rows, _ = ya.shape
    faces, _ = face_starts(rows // RIM)
    for k in range(n):
        for out, face in ((ca, faces[0]), (cb, faces[1])):
            for i in range(RIM):
                row = pl.ds(RIM * (face + i), RIM)
                out[k, pl.ds(RIM * i, RIM), :] = ya[k, row, :]
                out[k, pl.ds(SECOND + RIM * i, RIM), :] = yb[k, row, :]


def corner_faces(ya, yb, token):
    return pl.pallas_call(
        corner_kernel,
        in_specs=[INSIDE] * 3,
        out_specs=[INSIDE] * 2,
        out_shape=[shapes(ya.shape[0], 3 * ROWS, LANES)] * 2,
        name="corner_faces",
        compiler_params=pltpu.CompilerParams(vmem_limit_bytes=4 * MIB),
    )(ya, yb, token)


def sweeps_kernel(f0_in, xa, xb, ya, yb, ca, cb, route_ref, perm_ref, zmean_ref, f0, out_hbm, *rest):
    slot_refs, (f1, step, sgn, sem) = rest[:-4], rest[-4:]
    nx, ny, nz = out_hbm.shape
    n = nz // LANES
    nb = ny // ROWS
    copies = Copies(sem)
    _, rims = face_starts(nx)
    upper = first_is_above("narrow")
    parts = pieces(nx)
    for block, rim in ((xa, rims[0]), (xb, rims[1])):
        for k, lanes in lane_chunks(nz):
            copies.start("rim", block.at[:, :, lanes], f0.at[pl.ds(rim, RIM), k, pl.ds(ROWS, ny), :])
    place_rows(f0, RIM, nx, upper, ya, yb, ny)
    place_rows(f0, rims[0], RIM, upper, ca, ca, ny, SECOND)
    place_rows(f0, rims[1], RIM, upper, cb, cb, ny, SECOND)
    copies.wait("rim")

    def sweep(src, dst, x_first, x_end, y_first, blocks, mode):
        def plane(x, carry):
            for b in range(blocks):
                y = ROWS + y_first + b * ROWS
                ys = pl.ds(y, ROWS)
                f = [src[x, k, ys, :] for k in range(n)]
                fp = rolled(f, 1, lambda k: f[k])
                fm = rolled(f, -1, lambda k: f[k])
                for k in range(n):
                    if mode == "first":
                        st = (PSEUDO_STEP * f[k]) * lax.rsqrt(f[k] * f[k] + 1.0)
                        sg = jnp.where(f[k] > 0, 1.0, -1.0)
                        step[x, k, ys, :] = st
                        sgn[x, k, ys, :] = sg
                    else:
                        st = step[x, k, ys, :]
                        sg = sgn[x, k, ys, :]
                    p = sg * f[k]

                    def term(lo, hi):
                        m = jnp.maximum(p - jnp.minimum(sg * lo, sg * hi), 0.0)
                        return m * m

                    sq = term(src[x - 1, k, ys, :], src[x + 1, k, ys, :])
                    sq = sq + term(src[x, k, pl.ds(y - 1, ROWS), :], src[x, k, pl.ds(y + 1, ROWS), :])
                    sq = sq + term(fm[k], fp[k])
                    root = sq * lax.rsqrt(jnp.maximum(sq, 1e-30))
                    new = f[k] - st * (root - 1.0)
                    dst[x, k, ys, :] = new
                    if mode == "last":
                        sgn[x, k, ys, :] = new * lax.rsqrt(new * new + 1.0)
            return carry

        lax.fori_loop(x_first, x_end, plane, 0)

    sweep(f0, f1, 1, nx + 5, -2, nb + 1, "first")
    sweep(f1, f0, 2, nx + 4, -1, nb + 1, "middle")
    for x0, count in parts:
        sweep(f0, f1, RIM + x0, RIM + x0 + count, 0, nb, "last")
        for k, lanes in lane_chunks(nz):
            copies.start("out", f1.at[pl.ds(RIM + x0, count), k, pl.ds(ROWS, ny), :], out_hbm.at[pl.ds(x0, count), :, lanes])

    half = TILE // 2
    tz = nz // TILE
    blocks = [(tx, ty) for tx in range(nx // TILE) for ty in range(ny // TILE)]

    def two(a):
        high = a.astype(jnp.bfloat16)
        return high, (a - high.astype(jnp.float32)).astype(jnp.bfloat16)

    summed = []
    for tx, ty in blocks:
        for cx in range(half):
            row = []
            for k in range(n):
                x, y = RIM + tx * TILE + 2 * cx, ROWS + ty * TILE
                even, odd = pl.ds(y, half, 2), pl.ds(y + 1, half, 2)
                row.append((sgn[x, k, even, :] + sgn[x, k, odd, :]) + (sgn[x + 1, k, even, :] + sgn[x + 1, k, odd, :]))
            summed.append(jnp.concatenate(row, axis=1))
    summed = jnp.concatenate(summed, axis=0)
    zm = zmean_ref[...]
    dims = (((1,), (1,)), ((), ()))
    high, low = two(summed)
    mean = lax.dot_general(zm, high, dims, preferred_element_type=jnp.float32)
    mean = mean + lax.dot_general(zm, low, dims, preferred_element_type=jnp.float32)
    area = half * half
    tiles = jnp.concatenate(
        [
            jnp.concatenate([mean[c * tz : (c + 1) * tz, i * area : (i + 1) * area] for c in range(half)], axis=1)
            for i in range(len(blocks))
        ],
        axis=0,
    )
    pm = perm_ref[...]
    high, low = two(tiles)
    tiles = 0.5 - (jnp.dot(high, pm, preferred_element_type=jnp.float32) + jnp.dot(low, pm, preferred_element_type=jnp.float32))
    owners = len(slot_refs)
    capacity = slot_refs[0].shape[0]
    count = len(blocks) * tz
    route = route_ref[...] - lax.axis_index("wide")
    route = jnp.where(route < 0, route + owners, route)
    padded = -(-owners // ROWS) * ROWS
    matches = lax.broadcasted_iota(jnp.int32, (padded, count), 0) == route
    ordered = lax.broadcasted_iota(jnp.int32, (count, count), 0) < lax.broadcasted_iota(jnp.int32, (count, count), 1)
    match = jnp.where(matches, 1.0, 0.0)
    earlier = jnp.dot(
        match.astype(jnp.bfloat16), jnp.where(ordered, 1.0, 0.0).astype(jnp.bfloat16), preferred_element_type=jnp.float32
    )
    position = jnp.sum(earlier * match, axis=0, keepdims=True).astype(jnp.int32)
    target = route * capacity + position
    slots = lax.broadcasted_iota(jnp.int32, (owners * capacity, count), 0)
    pick = jnp.where(slots == target, 1.0, 0.0).astype(jnp.bfloat16)
    high, low = two(tiles)
    packed = jnp.dot(pick, high, preferred_element_type=jnp.float32) + jnp.dot(pick, low, preferred_element_type=jnp.float32)
    for i, ref in enumerate(slot_refs):
        ref[...] = packed[i * capacity : (i + 1) * capacity, :]
    copies.finish()


def sweeps(shape, moved, rims, route, owners, capacity):
    nx, ny, nz = shape
    half = TILE // 2
    tz = nz // TILE
    r = np.arange(half * tz)
    z = np.arange(nz)
    zmean = ((z[None, :] // TILE == (r % tz)[:, None]) & ((z[None, :] % TILE) // 2 == (r // tz)[:, None])) / 16.0
    src = np.arange(half**3)
    perm = np.zeros((half**3, half**3))
    perm[src, (src % half**2) * half + src // half**2] = 1.0
    return pl.pallas_call(
        sweeps_kernel,
        in_specs=[INSIDE] + [ANY] * 2 + [INSIDE] * 7,
        out_specs=[INSIDE, ANY] + [INSIDE] * owners,
        out_shape=[rimmed(shape), shapes(nx, ny, nz)] + [shapes(capacity, half**3)] * owners,
        input_output_aliases={0: 0},
        scratch_shapes=[rimmed(shape)] * 3 + [pltpu.SemaphoreType.DMA((64,))],
        name="sweeps",
        cost_estimate=estimate(shapes(*shape), 100),
        compiler_params=pltpu.CompilerParams(vmem_limit_bytes=30 * MIB),
    )(moved, *rims, route, jnp.asarray(perm, jnp.bfloat16), jnp.asarray(zmean, jnp.bfloat16))


def faces_kernel(core, xa_hbm, xb_hbm, ya_hbm, yb_hbm, x, rows, y, sem):
    nx, ny, nz = core.shape
    copies = Copies(sem)
    faces, _ = face_starts(nx)
    upper = first_is_above("narrow")
    groups = pieces(nx)
    copies.start("xa", core.at[pl.ds(faces[0], RIM)], x.at[0])
    copies.start("xb", core.at[pl.ds(faces[1], RIM)], x.at[1])
    for x0, count in groups:
        xs = pl.ds(x0, count)
        copies.start(x0, core.at[xs, pl.ds(0, ROWS), :], rows.at[0, xs])
        copies.start(x0, core.at[xs, pl.ds(ny - ROWS, ROWS), :], rows.at[1, xs])
    copies.wait("xa")
    copies.start("out", x.at[0], xa_hbm)
    copies.wait("xb")
    copies.start("out", x.at[1], xb_hbm)

    def plane(i, carry):
        for k, lanes in lane_chunks(nz):
            lo, hi = rows[0, i, pl.ds(0, RIM), lanes], rows[1, i, pl.ds(ROWS - RIM, RIM), lanes]
            y[0, k, pl.ds(RIM * i, RIM), :] = jnp.where(upper, hi, lo)
            y[1, k, pl.ds(RIM * i, RIM), :] = jnp.where(upper, lo, hi)
        return carry

    for x0, count in groups:
        side = pl.ds(RIM * x0, RIM * count)
        copies.wait(x0)
        lax.fori_loop(x0, x0 + count, plane, 0)
        copies.start("out", y.at[0, :, side], ya_hbm.at[:, side])
        copies.start("out", y.at[1, :, side], yb_hbm.at[:, side])
    copies.finish()


def own_faces(block):
    nx, ny, nz = block.shape
    f32 = jnp.float32
    return pl.pallas_call(
        faces_kernel,
        in_specs=[ANY],
        out_specs=[ANY] * 4,
        out_shape=[shapes(RIM, ny, nz)] * 2 + [shapes(*side_shape(block.shape))] * 2,
        scratch_shapes=[
            pltpu.VMEM((2, RIM, ny, nz), f32),
            pltpu.VMEM((2, nx, ROWS, nz), f32),
            pltpu.VMEM((2,) + side_shape(block.shape), f32),
            pltpu.SemaphoreType.DMA((24,)),
        ],
        name="own_faces",
        compiler_params=pltpu.CompilerParams(vmem_limit_bytes=61 * MIB),
    )(block)


def gather_kernel(*refs):
    blocks, out, sem = refs[:-2], refs[-2], refs[-1]
    me, owners = lax.axis_index("wide"), len(blocks)
    copies = [
        pltpu.make_async_copy(b, out.at[lax.rem(me - i + owners, owners)], sem.at[i]) for i, b in enumerate(blocks)
    ]
    for c in copies:
        c.start()
    for c in copies:
        c.wait()


def gather_blocks(blocks):
    return pl.pallas_call(
        gather_kernel,
        in_specs=[INSIDE] * len(blocks),
        out_specs=ANY,
        out_shape=shapes(len(blocks), *blocks[0].shape),
        scratch_shapes=[pltpu.SemaphoreType.DMA((len(blocks),))],
        name="gather_blocks",
        compiler_params=pltpu.CompilerParams(vmem_limit_bytes=8 * MIB),
    )(*blocks)


def trade(axis, first, second):
    peers = lax.axis_size(axis)
    return (
        lax.ppermute(first, axis, [(i, i ^ 1) for i in range(peers)]),
        lax.ppermute(second, axis, [(i, (i + 1 if i % 2 else i - 1) % peers) for i in range(peers)]),
    )


def on_device(level_set, velocity, box_owner):
    owners = lax.axis_size("wide")
    xa, xb, ya, yb = own_faces(level_set)
    xa, xb = trade("wide", xa, xb)
    ya, yb = trade("narrow", ya, yb)
    field, acc, u = along_z(level_set, velocity)
    shape = level_set.shape
    field, acc, yf_a, yf_b = edge_rows(shape, field, acc, u, xa, xb, ya, yb)
    ya, yb = trade("narrow", yf_a, yf_b)
    acc, bx_a, bx_b = edge_planes(shape, acc, field, u)
    xa, xb = trade("wide", bx_a, bx_b)
    acc, token = interior_y(shape, acc, field, u, bx_a)
    ca, cb = trade("wide", *corner_faces(ya, yb, token))
    moved = interior_x(shape, acc, field, u)
    tile_count = box_owner.shape[2]
    capacity = max(2, 5 * tile_count // (2 * owners))
    route = box_owner.reshape(1, tile_count)
    _, surface, *slots = sweeps(shape, moved, (xa, xb, ya, yb, ca, cb), route, owners, capacity)
    received = [slots[0]]
    for step in range(1, owners):
        received.append(lax.ppermute(slots[step], "wide", [(i, (i + step) % owners) for i in range(owners)]))
    box_slots = gather_blocks(received)
    return (surface, box_slots.reshape(1, 1, owners * capacity, -1))


def solution(mesh):
    return jax.shard_map(
        on_device,
        mesh=mesh,
        in_specs=(
            P("wide", "narrow", None),
            P(None, "wide", "narrow", None),
            P("wide", "narrow", None, None),
        ),
        out_specs=(P("wide", "narrow", None), P("wide", "narrow", None, None)),
        check_vma=False,
    )
```

```python
import math
import jax
import jax.numpy as jnp
import numpy as np
from jax import lax
from jax.experimental import pallas as pl
from jax.experimental.pallas import tpu as pltpu
from jax.sharding import PartitionSpec as P

TILE = 16
WENO_EPS = 1e-06
PSEUDO_STEP = 0.3
RIM = 3
SECOND = 12
LANES = 128
ROWS = 8
MIB = 1024 * 1024


def correction(s1, s2, s3, h1, h0):
    r1 = 1.0 / s1
    r2 = 1.0 / s2
    r3 = 1.0 / s3
    w1 = (r1 * r1) * (1.0 / 3.0)
    w2 = (r2 * r2) * 2.0
    w3 = r3 * r3
    return (w1 * (4.0 * h1 - h0) + (w3 - w2) * h0) / ((w1 + w3) + w2)


def pair_forms(x, y, t):
    t2 = t + t
    q = t * t + 0.75 * WENO_EPS
    y75 = 0.75 * y
    w = q + y75 * x
    u = w + y75 * t2
    v = w - (0.75 * x) * t2
    return u, w, v


def rolled(chunks, shift, fill):
    lane = lax.broadcasted_iota(jnp.int32, chunks[0].shape, 1)
    turned = [pltpu.roll(c, (-shift) % LANES, 1) for c in chunks]
    out = []
    n = len(chunks)
    for k in range(n):
        other = k + (1 if shift > 0 else -1)
        beyond = turned[other] if 0 <= other < n else fill(k)
        mask = lane >= LANES - shift if shift > 0 else lane < -shift
        out.append(jnp.where(mask, beyond, turned[k]))
    return out


def along_z_kernel(core, u_hbm, field, acc, u, uz, ft, ut, es, us, ws, vs, hs, sem):
    nx, ny, nz = core.shape
    copies = Copies(sem)
    per = LANES // ny
    step = 2 * per
    bounds = [0, step, 2 * step, nx // 2, nx]
    groups = [(x0, x1) for x0, x1 in zip(bounds, bounds[1:]) if x1 > x0]
    for x0, x1 in groups:
        xs = pl.ds(x0, x1 - x0)
        for k, lanes in lane_chunks(nz):
            copies.start(x0, core.at[xs, :, lanes], field.at[pl.ds(x0 + RIM, x1 - x0), k, pl.ds(ROWS, ny), :])
        copies.start(x0, u_hbm.at[2, xs], uz.at[xs])
    copies.start("u", u_hbm.at[pl.ds(0, 2)], u)
    streams = (es, us, ws, vs, hs)
    first, second = (ft.at[0], ut.at[0]), (ft.at[1], ut.at[1])

    def two(j, carry):
        turn_in(field, uz, *second, per, 2 * j + 1)
        z_planes(field, acc, *first, streams, per, 2 * j)
        turn_in(field, uz, *first, per, jnp.minimum(2 * j + 2, nx // per - 1))
        z_planes(field, acc, *second, streams, per, 2 * j + 1)
        return carry

    copies.wait(0)
    turn_in(field, uz, *first, per, 0)
    for g, (x0, x1) in enumerate(groups):
        if g + 1 < len(groups):
            copies.wait(groups[g + 1][0])
        lax.fori_loop(x0 // step, x1 // step, two, 0)
    copies.finish()


def turn_in(field, uz, ft, ut, per, i):
    ny = LANES // per
    n = field.shape[1]
    depth = n * LANES
    rows = pl.ds(ROWS, ny)
    planes = [per * i + p for p in range(per)]
    for k in range(n):
        ft[pl.ds(ROWS + k * LANES, LANES), :] = jnp.concatenate([field[x + RIM, k, rows, :] for x in planes], axis=0).T
        v = jnp.concatenate([uz[x, :, pl.ds(k * LANES, LANES)] for x in planes], axis=0)
        ut[pl.ds(k * LANES, LANES), :] = v.astype(jnp.float32).T
    ft[pl.ds(0, ROWS), :] = jnp.broadcast_to(ft[pl.ds(ROWS, 1), :], (ROWS, LANES))
    ft[pl.ds(ROWS + depth, ROWS), :] = jnp.broadcast_to(ft[pl.ds(ROWS + depth - 1, 1), :], (ROWS, LANES))


def z_planes(field, acc, ft, ut, streams, per, i):
    es, us, ws, vs, hs = streams
    ny = LANES // per
    n = field.shape[1]
    depth = n * LANES
    rows = pl.ds(ROWS, ny)
    planes = [per * i + p for p in range(per)]

    def at(z):
        return ft[pl.ds(ROWS + z, ROWS), :]

    blocks = depth // ROWS
    for b in range(blocks + 1):
        z = b * ROWS - 2
        f0 = at(z)
        es[pl.ds(ROWS + b * ROWS, ROWS), :] = (at(z + 1) - f0) - (f0 - at(z - 1))
    for b in range(blocks + 1):
        r = ROWS + b * ROWS
        e0, e1, e_1 = es[pl.ds(r, ROWS), :], es[pl.ds(r + 1, ROWS), :], es[pl.ds(r - 1, ROWS), :]
        t = e1 - e0
        us[pl.ds(r, ROWS), :], ws[pl.ds(r, ROWS), :], vs[pl.ds(r, ROWS), :] = pair_forms(e0, e1, t)
        hs[pl.ds(r, ROWS), :] = t - (e0 - e_1)
    for b in range(blocks):

        def of(ref, d):
            return ref[pl.ds(ROWS + b * ROWS + 2 + d, ROWS), :]

        zs = pl.ds(b * ROWS, ROWS)
        v = ut[zs, :]
        up = v > 0
        s1 = jnp.where(up, of(us, -2), of(vs, 1))
        s2 = jnp.where(up, of(ws, -1), of(ws, 0))
        s3 = jnp.where(up, of(vs, 0), of(us, -1))
        h1 = jnp.where(up, of(hs, -1), of(hs, 1))
        phi = correction(s1, s2, s3, h1, of(hs, 0))
        mid = 6.0 * (at(b * ROWS + 1) - at(b * ROWS - 1)) - (of(es, 1) - of(es, -1))
        v12 = v * (1.0 / 12.0)
        ut[zs, :] = v12 * mid - jnp.abs(v12) * phi
    for k in range(n):
        change = ut[pl.ds(k * LANES, LANES), :].T
        for p, x in enumerate(planes):
            acc[x + RIM, k, rows, :] = field[x + RIM, k, rows, :] - change[p * ny : (p + 1) * ny, :]


def in_vmem(shape, dtype=jnp.float32):
    return pltpu.VMEM(shape, dtype)


def rimmed(shape):
    nx, ny, nz = shape
    return in_vmem((nx + 2 * RIM, nz // LANES, ny + 2 * ROWS, LANES))


def along_z(level_set, velocity):
    nx, ny, nz = level_set.shape
    return pl.pallas_call(
        along_z_kernel,
        in_specs=[ANY, ANY],
        out_specs=[INSIDE] * 3,
        out_shape=[rimmed(level_set.shape)] * 2 + [in_vmem((2, nx, ny, nz), velocity.dtype)],
        scratch_shapes=[
            pltpu.VMEM((nx, ny, nz), velocity.dtype),
            pltpu.VMEM((2, nz + 2 * ROWS, LANES), jnp.float32),
            pltpu.VMEM((2, nz, LANES), jnp.float32),
        ]
        + [pltpu.VMEM((nz + 3 * ROWS, LANES), jnp.float32)] * 5
        + [pltpu.SemaphoreType.DMA((40,))],
        name="along_z",
        cost_estimate=estimate(level_set, 60),
        compiler_params=pltpu.CompilerParams(vmem_limit_bytes=46 * MIB),
    )(level_set, velocity)


def estimate(block, flops):
    return pl.CostEstimate(flops=flops * block.size, bytes_accessed=8 * block.size, transcendentals=4 * block.size)


class Copies:
    def __init__(self, sem):
        self.sem, self.used, self.groups = sem, 0, {}

    def start(self, group, src, dst):
        copy = pltpu.make_async_copy(src, dst, self.sem.at[self.used])
        self.used += 1
        copy.start()
        self.groups.setdefault(group, []).append(copy)

    def wait(self, group):
        for copy in self.groups.pop(group, ()):
            copy.wait()

    def finish(self):
        for group in list(self.groups):
            self.wait(group)


def lane_chunks(nz):
    return [(k, pl.ds(k * LANES, LANES)) for k in range(nz // LANES)]


def x_column(field, u, acc, k, yb, ranges):
    ys = pl.ds(pl.multiple_of(yb * ROWS, ROWS), ROWS)
    yf = pl.ds(pl.multiple_of(yb * ROWS + ROWS, ROWS), ROWS)
    lanes = pl.ds(pl.multiple_of(k * LANES, LANES), LANES)
    for first, last in ranges:
        f, g, e, t, h, pu, pw, pv = {}, {}, {}, {}, {}, {}, {}, {}

        def value(x):
            f[x] = field[x + RIM, k, yf, :]
            if x - 1 in f:
                g[x - 1] = f[x] - f[x - 1]
            if x - 2 in g:
                e[x - 1] = g[x - 1] - g[x - 2]
            if x - 2 in e:
                t[x - 2] = e[x - 1] - e[x - 2]
                pu[x - 2], pw[x - 2], pv[x - 2] = pair_forms(e[x - 2], e[x - 1], t[x - 2])
            if x - 3 in t:
                h[x - 2] = t[x - 2] - t[x - 3]

        for x in range(first - RIM, first + RIM):
            value(x)
        for x in range(first, last):
            value(x + RIM)
            v = u[0, x, ys, lanes].astype(jnp.float32)
            up = v > 0
            s1 = jnp.where(up, pu[x - 2], pv[x + 1])
            s2 = jnp.where(up, pw[x - 1], pw[x])
            s3 = jnp.where(up, pv[x], pu[x - 1])
            h1 = jnp.where(up, h[x - 1], h[x + 1])
            phi = correction(s1, s2, s3, h1, h[x])
            mid = 6.0 * (g[x] + g[x - 1]) - (e[x + 1] - e[x - 1])
            v12 = v * (1.0 / 12.0)
            acc[x + RIM, k, yf, :] = acc[x + RIM, k, yf, :] - (v12 * mid - jnp.abs(v12) * phi)


def y_plane(field, u, acc, streams, x, n, ranges):
    es, us, ws, vs, hs = streams
    for k in range(n):
        lanes = pl.ds(k * LANES, LANES)

        def at(y):
            return field[x + RIM, k, pl.ds(ROWS + y, ROWS), :]

        for first, last in ranges:
            for b in range(first, last + 1):
                y = b * ROWS - 2
                f0 = at(y)
                es[k, pl.ds(ROWS + b * ROWS, ROWS), :] = (at(y + 1) - f0) - (f0 - at(y - 1))
            for b in range(first, last + 1):
                r = ROWS + b * ROWS
                e0, e1, e_1 = es[k, pl.ds(r, ROWS), :], es[k, pl.ds(r + 1, ROWS), :], es[k, pl.ds(r - 1, ROWS), :]
                t = e1 - e0
                us[k, pl.ds(r, ROWS), :], ws[k, pl.ds(r, ROWS), :], vs[k, pl.ds(r, ROWS), :] = pair_forms(e0, e1, t)
                hs[k, pl.ds(r, ROWS), :] = t - (e0 - e_1)
            for b in range(first, last):
                ys, yf = pl.ds(b * ROWS, ROWS), pl.ds(b * ROWS + ROWS, ROWS)

                def of(ref, d):
                    return ref[k, pl.ds(ROWS + b * ROWS + 2 + d, ROWS), :]

                v = u[1, x, ys, lanes].astype(jnp.float32)
                up = v > 0
                s1 = jnp.where(up, of(us, -2), of(vs, 1))
                s2 = jnp.where(up, of(ws, -1), of(ws, 0))
                s3 = jnp.where(up, of(vs, 0), of(us, -1))
                h1 = jnp.where(up, of(hs, -1), of(hs, 1))
                phi = correction(s1, s2, s3, h1, of(hs, 0))
                mid = 6.0 * (at(b * ROWS + 1) - at(b * ROWS - 1)) - (of(es, 1) - of(es, -1))
                v12 = v * (1.0 / 12.0)
                acc[x + RIM, k, yf, :] = acc[x + RIM, k, yf, :] - (v12 * mid - jnp.abs(v12) * phi)


def place_rows(field, x0, count, upper, first, second, ny, second_at=0):
    n = field.shape[1]

    def body(i, carry):
        for k in range(n):
            one = first[k, pl.ds(RIM * i, RIM), :]
            two = second[k, pl.ds(second_at + RIM * i, RIM), :]
            field[i + x0, k, pl.ds(ROWS - RIM, RIM), :] = jnp.where(upper, two, one)
            field[i + x0, k, pl.ds(ROWS + ny, RIM), :] = jnp.where(upper, one, two)
        return carry

    lax.fori_loop(0, count, body, 0)


def side_shape(shape):
    nx, _, nz = shape
    return (nz // LANES, RIM * nx + ROWS, LANES)


def first_is_above(axis):
    return lax.rem(lax.axis_index(axis), 2) == 0


def face_starts(nx):
    even = first_is_above("wide")
    faces = (jnp.where(even, nx - RIM, 0), jnp.where(even, 0, nx - RIM))
    rims = (jnp.where(even, nx + RIM, 0), jnp.where(even, 0, nx + RIM))
    return faces, rims


def pieces(nx):
    count = math.gcd(nx, 4)
    return [(i * (nx // count), nx // count) for i in range(count)]


def edge_rows_kernel(
    field_in, acc_in, u, xa, xb, ya_hbm, yb_hbm, field, acc, yfa_hbm, yfb_hbm, es, us, ws, vs, hs, ya, yb, yf_a, yf_b, sem
):
    _, nx, ny, nz = u.shape
    n, nb = nz // LANES, ny // ROWS
    copies = Copies(sem)
    streams = (es, us, ws, vs, hs)
    _, rims = face_starts(nx)
    upper = first_is_above("narrow")
    for block, rim in zip((xa, xb), rims):
        for k, lanes in lane_chunks(nz):
            copies.start("x", block.at[:, :, lanes], field.at[pl.ds(rim, RIM), k, pl.ds(ROWS, ny), :])
    copies.start("y", ya_hbm, ya)
    copies.start("y", yb_hbm, yb)
    copies.wait("x")

    def edge_column(i, carry):
        x_column(field, u, acc, lax.rem(i, n), lax.div(i, n) * (nb - 1), ((0, nx),))
        return carry

    lax.fori_loop(0, 2 * n, edge_column, 0)
    copies.wait("y")
    place_rows(field, RIM, nx, upper, ya, yb, ny)

    def edge_plane(x, carry):
        y_plane(field, u, acc, streams, x, n, ((0, 1), (nb - 1, nb)))
        for k in range(n):
            lo, hi = acc[x + RIM, k, pl.ds(ROWS, RIM), :], acc[x + RIM, k, pl.ds(ROWS + ny - RIM, RIM), :]
            yf_a[k, pl.ds(RIM * x, RIM), :] = jnp.where(upper, hi, lo)
            yf_b[k, pl.ds(RIM * x, RIM), :] = jnp.where(upper, lo, hi)
        return carry

    for x0, count in pieces(nx):
        rows = pl.ds(RIM * x0, RIM * count)
        lax.fori_loop(x0, x0 + count, edge_plane, 0)
        copies.start("out", yf_a.at[:, rows], yfa_hbm.at[:, rows])
        copies.start("out", yf_b.at[:, rows], yfb_hbm.at[:, rows])
    copies.finish()


def edge_planes_kernel(acc_in, field, u, acc, bx_a, bx_b, es, us, ws, vs, hs, sem):
    _, nx, ny, nz = u.shape
    n, nb = nz // LANES, ny // ROWS
    copies = Copies(sem)
    faces, _ = face_starts(nx)

    def both_ends(i, carry):
        y_plane(field, u, acc, (es, us, ws, vs, hs), jnp.where(i < RIM, i, nx - 2 * RIM + i), n, ((1, nb - 1),))
        return carry

    lax.fori_loop(0, 2 * RIM, both_ends, 0)

    def inner_column(i, carry):
        x_column(field, u, acc, lax.rem(i, n), 1 + lax.div(i, n), ((0, RIM), (nx - RIM, nx)))
        return carry

    lax.fori_loop(0, n * (nb - 2), inner_column, 0)
    rows = pl.ds(ROWS, ny)
    for face, out in zip(faces, (bx_a, bx_b)):
        for k, lanes in lane_chunks(nz):
            copies.start("out", acc.at[pl.ds(face + RIM, RIM), k, rows, :], out.at[:, :, lanes])
    copies.finish()


def interior_y_kernel(acc_in, field, u, after, acc, token, es, us, ws, vs, hs):
    _, nx, ny, nz = u.shape
    n, nb = nz // LANES, ny // ROWS

    def rows(x, carry):
        y_plane(field, u, acc, (es, us, ws, vs, hs), x, n, ((1, nb - 1),))
        return carry

    lax.fori_loop(RIM, nx - RIM, rows, 0)
    token[...] = jnp.zeros_like(token)


def interior_x_kernel(acc_in, field, u, acc):
    _, nx, ny, nz = u.shape
    n, nb = nz // LANES, ny // ROWS

    def column(i, carry):
        x_column(field, u, acc, lax.rem(i, n), 1 + lax.div(i, n), ((RIM, nx - RIM),))
        return carry

    lax.fori_loop(0, n * (nb - 2), column, 0)


ANY = pl.BlockSpec(memory_space=pl.ANY)
INSIDE = pl.BlockSpec(memory_space=pltpu.VMEM)


def stream_scratch(nx, ny, nz):
    return [pltpu.VMEM((nz // LANES, ny + 3 * ROWS, LANES), jnp.float32)] * 5


def shapes(*dims):
    return jax.ShapeDtypeStruct(dims, jnp.float32)


def edge_rows(shape, field, acc, u, xa, xb, ya, yb):
    nx, ny, nz = shape
    return pl.pallas_call(
        edge_rows_kernel,
        in_specs=[INSIDE] * 3 + [ANY] * 4,
        out_specs=[INSIDE] * 2 + [ANY] * 2,
        out_shape=[rimmed(shape)] * 2 + [shapes(*side_shape(shape))] * 2,
        input_output_aliases={0: 0, 1: 1},
        scratch_shapes=stream_scratch(nx, ny, nz)
        + [pltpu.VMEM(side_shape(shape), jnp.float32)] * 4
        + [pltpu.SemaphoreType.DMA((24,))],
        name="edge_rows",
        cost_estimate=estimate(shapes(*shape), 30),
        compiler_params=pltpu.CompilerParams(vmem_limit_bytes=8 * MIB),
    )(field, acc, u, xa, xb, ya, yb)


def edge_planes(shape, acc, field, u):
    nx, ny, nz = shape
    return pl.pallas_call(
        edge_planes_kernel,
        in_specs=[INSIDE] * 3,
        out_specs=[INSIDE] + [ANY] * 2,
        out_shape=[rimmed(shape)] + [shapes(RIM, ny, nz)] * 2,
        input_output_aliases={0: 0},
        scratch_shapes=stream_scratch(nx, ny, nz) + [pltpu.SemaphoreType.DMA((8,))],
        name="edge_planes",
        cost_estimate=estimate(shapes(*shape), 20),
        compiler_params=pltpu.CompilerParams(vmem_limit_bytes=4 * MIB),
    )(acc, field, u)


def interior_y(shape, acc, field, u, after):
    return pl.pallas_call(
        interior_y_kernel,
        in_specs=[INSIDE] * 3 + [ANY],
        out_specs=[INSIDE] * 2,
        out_shape=[rimmed(shape), shapes(ROWS, LANES)],
        input_output_aliases={0: 0},
        scratch_shapes=stream_scratch(*shape),
        name="interior_y",
        cost_estimate=estimate(shapes(*shape), 30),
        compiler_params=pltpu.CompilerParams(vmem_limit_bytes=4 * MIB),
    )(acc, field, u, after)


def interior_x(shape, acc, field, u):
    return pl.pallas_call(
        interior_x_kernel,
        in_specs=[INSIDE] * 3,
        out_specs=INSIDE,
        out_shape=rimmed(shape),
        input_output_aliases={0: 0},
        name="interior_x",
        cost_estimate=estimate(shapes(*shape), 30),
        compiler_params=pltpu.CompilerParams(vmem_limit_bytes=4 * MIB),
    )(acc, field, u)


def corner_kernel(ya, yb, token, ca, cb):
    n, rows, _ = ya.shape
    faces, _ = face_starts((rows - ROWS) // RIM)
    for k in range(n):
        for out, face in ((ca, faces[0]), (cb, faces[1])):
            for i in range(RIM):
                row = pl.ds(RIM * (face + i), RIM)
                out[k, pl.ds(RIM * i, RIM), :] = ya[k, row, :]
                out[k, pl.ds(SECOND + RIM * i, RIM), :] = yb[k, row, :]


def corner_faces(ya, yb, token):
    return pl.pallas_call(
        corner_kernel,
        in_specs=[INSIDE] * 3,
        out_specs=[INSIDE] * 2,
        out_shape=[shapes(ya.shape[0], 4 * ROWS, LANES)] * 2,
        name="corner_faces",
        compiler_params=pltpu.CompilerParams(vmem_limit_bytes=4 * MIB),
    )(ya, yb, token)


def sweeps_kernel(f0_in, xa, xb, ya, yb, ca, cb, route_ref, perm_ref, zmean_ref, f0, out_hbm, *rest):
    slot_refs, (f1, step, sgn, sem) = rest[:-4], rest[-4:]
    nx, ny, nz = out_hbm.shape
    n = nz // LANES
    nb = ny // ROWS
    copies = Copies(sem)
    _, rims = face_starts(nx)
    upper = first_is_above("narrow")
    parts = pieces(nx)
    for block, rim in ((xa, rims[0]), (xb, rims[1])):
        for k, lanes in lane_chunks(nz):
            copies.start("rim", block.at[:, :, lanes], f0.at[pl.ds(rim, RIM), k, pl.ds(ROWS, ny), :])
    place_rows(f0, RIM, nx, upper, ya, yb, ny)
    place_rows(f0, rims[0], RIM, upper, ca, ca, ny, SECOND)
    place_rows(f0, rims[1], RIM, upper, cb, cb, ny, SECOND)
    copies.wait("rim")

    def sweep(src, dst, x_first, x_end, y_first, blocks, mode):
        def plane(x, carry):
            for b in range(blocks):
                y = ROWS + y_first + b * ROWS
                ys = pl.ds(y, ROWS)
                f = [src[x, k, ys, :] for k in range(n)]
                fp = rolled(f, 1, lambda k: f[k])
                fm = rolled(f, -1, lambda k: f[k])
                for k in range(n):
                    if mode == "first":
                        st = (PSEUDO_STEP * f[k]) * lax.rsqrt(f[k] * f[k] + 1.0)
                        sg = jnp.where(f[k] > 0, 1.0, -1.0)
                        step[x, k, ys, :] = st
                        sgn[x, k, ys, :] = sg
                    else:
                        st = step[x, k, ys, :]
                        sg = sgn[x, k, ys, :]
                    p = sg * f[k]

                    def term(lo, hi):
                        m = jnp.maximum(p - jnp.minimum(sg * lo, sg * hi), 0.0)
                        return m * m

                    sq = term(src[x - 1, k, ys, :], src[x + 1, k, ys, :])
                    sq = sq + term(src[x, k, pl.ds(y - 1, ROWS), :], src[x, k, pl.ds(y + 1, ROWS), :])
                    sq = sq + term(fm[k], fp[k])
                    root = sq * lax.rsqrt(jnp.maximum(sq, 1e-30))
                    new = f[k] - st * (root - 1.0)
                    dst[x, k, ys, :] = new
                    if mode == "last":
                        sgn[x, k, ys, :] = new * lax.rsqrt(new * new + 1.0)
            return carry

        lax.fori_loop(x_first, x_end, plane, 0)

    sweep(f0, f1, 1, nx + 5, -2, nb + 1, "first")
    sweep(f1, f0, 2, nx + 4, -1, nb + 1, "middle")
    for x0, count in parts:
        sweep(f0, f1, RIM + x0, RIM + x0 + count, 0, nb, "last")
        for k, lanes in lane_chunks(nz):
            copies.start("out", f1.at[pl.ds(RIM + x0, count), k, pl.ds(ROWS, ny), :], out_hbm.at[pl.ds(x0, count), :, lanes])

    half = TILE // 2
    tz = nz // TILE
    blocks = [(tx, ty) for tx in range(nx // TILE) for ty in range(ny // TILE)]

    def two(a):
        high = a.astype(jnp.bfloat16)
        return high, (a - high.astype(jnp.float32)).astype(jnp.bfloat16)

    summed = []
    for tx, ty in blocks:
        for cx in range(half):
            row = []
            for k in range(n):
                x, y = RIM + tx * TILE + 2 * cx, ROWS + ty * TILE
                even, odd = pl.ds(y, half, 2), pl.ds(y + 1, half, 2)
                row.append((sgn[x, k, even, :] + sgn[x, k, odd, :]) + (sgn[x + 1, k, even, :] + sgn[x + 1, k, odd, :]))
            summed.append(jnp.concatenate(row, axis=1))
    summed = jnp.concatenate(summed, axis=0)
    zm = zmean_ref[...]
    dims = (((1,), (1,)), ((), ()))
    high, low = two(summed)
    mean = lax.dot_general(zm, high, dims, preferred_element_type=jnp.float32)
    mean = mean + lax.dot_general(zm, low, dims, preferred_element_type=jnp.float32)
    area = half * half
    tiles = jnp.concatenate(
        [
            jnp.concatenate([mean[c * tz : (c + 1) * tz, i * area : (i + 1) * area] for c in range(half)], axis=1)
            for i in range(len(blocks))
        ],
        axis=0,
    )
    pm = perm_ref[...]
    high, low = two(tiles)
    tiles = 0.5 - (jnp.dot(high, pm, preferred_element_type=jnp.float32) + jnp.dot(low, pm, preferred_element_type=jnp.float32))
    owners = len(slot_refs)
    capacity = slot_refs[0].shape[0]
    count = len(blocks) * tz
    route = route_ref[...] - lax.axis_index("wide")
    route = jnp.where(route < 0, route + owners, route)
    padded = -(-owners // ROWS) * ROWS
    matches = lax.broadcasted_iota(jnp.int32, (padded, count), 0) == route
    ordered = lax.broadcasted_iota(jnp.int32, (count, count), 0) < lax.broadcasted_iota(jnp.int32, (count, count), 1)
    match = jnp.where(matches, 1.0, 0.0)
    earlier = jnp.dot(
        match.astype(jnp.bfloat16), jnp.where(ordered, 1.0, 0.0).astype(jnp.bfloat16), preferred_element_type=jnp.float32
    )
    position = jnp.sum(earlier * match, axis=0, keepdims=True).astype(jnp.int32)
    target = route * capacity + position
    slots = lax.broadcasted_iota(jnp.int32, (owners * capacity, count), 0)
    pick = jnp.where(slots == target, 1.0, 0.0).astype(jnp.bfloat16)
    high, low = two(tiles)
    packed = jnp.dot(pick, high, preferred_element_type=jnp.float32) + jnp.dot(pick, low, preferred_element_type=jnp.float32)
    for i, ref in enumerate(slot_refs):
        ref[...] = packed[i * capacity : (i + 1) * capacity, :]
    copies.finish()


def sweeps(shape, moved, rims, route, owners, capacity):
    nx, ny, nz = shape
    half = TILE // 2
    tz = nz // TILE
    r = np.arange(half * tz)
    z = np.arange(nz)
    zmean = ((z[None, :] // TILE == (r % tz)[:, None]) & ((z[None, :] % TILE) // 2 == (r // tz)[:, None])) / 16.0
    src = np.arange(half**3)
    perm = np.zeros((half**3, half**3))
    perm[src, (src % half**2) * half + src // half**2] = 1.0
    return pl.pallas_call(
        sweeps_kernel,
        in_specs=[INSIDE] + [ANY] * 2 + [INSIDE] * 7,
        out_specs=[INSIDE, ANY] + [INSIDE] * owners,
        out_shape=[rimmed(shape), shapes(nx, ny, nz)] + [shapes(capacity, half**3)] * owners,
        input_output_aliases={0: 0},
        scratch_shapes=[rimmed(shape)] * 3 + [pltpu.SemaphoreType.DMA((64,))],
        name="sweeps",
        cost_estimate=estimate(shapes(*shape), 100),
        compiler_params=pltpu.CompilerParams(vmem_limit_bytes=30 * MIB),
    )(moved, *rims, route, jnp.asarray(perm, jnp.bfloat16), jnp.asarray(zmean, jnp.bfloat16))


def faces_kernel(core, xa_hbm, xb_hbm, ya_hbm, yb_hbm, x, rows, y, sem):
    nx, ny, nz = core.shape
    copies = Copies(sem)
    faces, _ = face_starts(nx)
    upper = first_is_above("narrow")
    groups = pieces(nx)
    copies.start("xa", core.at[pl.ds(faces[0], RIM)], x.at[0])
    copies.start("xb", core.at[pl.ds(faces[1], RIM)], x.at[1])
    for x0, count in groups:
        xs = pl.ds(x0, count)
        copies.start(x0, core.at[xs, pl.ds(0, ROWS), :], rows.at[0, xs])
        copies.start(x0, core.at[xs, pl.ds(ny - ROWS, ROWS), :], rows.at[1, xs])
    copies.wait("xa")
    copies.start("out", x.at[0], xa_hbm)
    copies.wait("xb")
    copies.start("out", x.at[1], xb_hbm)

    def plane(i, carry):
        for k, lanes in lane_chunks(nz):
            lo, hi = rows[0, i, pl.ds(0, RIM), lanes], rows[1, i, pl.ds(ROWS - RIM, RIM), lanes]
            y[0, k, pl.ds(RIM * i, RIM), :] = jnp.where(upper, hi, lo)
            y[1, k, pl.ds(RIM * i, RIM), :] = jnp.where(upper, lo, hi)
        return carry

    for x0, count in groups:
        side = pl.ds(RIM * x0, RIM * count)
        copies.wait(x0)
        lax.fori_loop(x0, x0 + count, plane, 0)
        copies.start("out", y.at[0, :, side], ya_hbm.at[:, side])
        copies.start("out", y.at[1, :, side], yb_hbm.at[:, side])
    copies.finish()


def own_faces(block):
    nx, ny, nz = block.shape
    f32 = jnp.float32
    return pl.pallas_call(
        faces_kernel,
        in_specs=[ANY],
        out_specs=[ANY] * 4,
        out_shape=[shapes(RIM, ny, nz)] * 2 + [shapes(*side_shape(block.shape))] * 2,
        scratch_shapes=[
            pltpu.VMEM((2, RIM, ny, nz), f32),
            pltpu.VMEM((2, nx, ROWS, nz), f32),
            pltpu.VMEM((2,) + side_shape(block.shape), f32),
            pltpu.SemaphoreType.DMA((24,)),
        ],
        name="own_faces",
        compiler_params=pltpu.CompilerParams(vmem_limit_bytes=61 * MIB),
    )(block)


def gather_kernel(*refs):
    blocks, out, sem = refs[:-2], refs[-2], refs[-1]
    me, owners = lax.axis_index("wide"), len(blocks)
    copies = [
        pltpu.make_async_copy(b, out.at[lax.rem(me - i + owners, owners)], sem.at[i]) for i, b in enumerate(blocks)
    ]
    for c in copies:
        c.start()
    for c in copies:
        c.wait()


def gather_blocks(blocks):
    return pl.pallas_call(
        gather_kernel,
        in_specs=[INSIDE] * len(blocks),
        out_specs=ANY,
        out_shape=shapes(len(blocks), *blocks[0].shape),
        scratch_shapes=[pltpu.SemaphoreType.DMA((len(blocks),))],
        name="gather_blocks",
        compiler_params=pltpu.CompilerParams(vmem_limit_bytes=8 * MIB),
    )(*blocks)


def trade(axis, first, second):
    peers = lax.axis_size(axis)
    return (
        lax.ppermute(first, axis, [(i, i ^ 1) for i in range(peers)]),
        lax.ppermute(second, axis, [(i, (i + 1 if i % 2 else i - 1) % peers) for i in range(peers)]),
    )


def on_device(level_set, velocity, box_owner):
    owners = lax.axis_size("wide")
    xa, xb, ya, yb = own_faces(level_set)
    xa, xb = trade("wide", xa, xb)
    ya, yb = trade("narrow", ya, yb)
    field, acc, u = along_z(level_set, velocity)
    shape = level_set.shape
    field, acc, yf_a, yf_b = edge_rows(shape, field, acc, u, xa, xb, ya, yb)
    ya, yb = trade("narrow", yf_a, yf_b)
    acc, bx_a, bx_b = edge_planes(shape, acc, field, u)
    xa, xb = trade("wide", bx_a, bx_b)
    acc, token = interior_y(shape, acc, field, u, bx_a)
    ca, cb = trade("wide", *corner_faces(ya, yb, token))
    moved = interior_x(shape, acc, field, u)
    tile_count = box_owner.shape[2]
    capacity = max(2, 5 * tile_count // (2 * owners))
    route = box_owner.reshape(1, tile_count)
    _, surface, *slots = sweeps(shape, moved, (xa, xb, ya, yb, ca, cb), route, owners, capacity)
    received = [slots[0]]
    for step in range(1, owners):
        received.append(lax.ppermute(slots[step], "wide", [(i, (i + step) % owners) for i in range(owners)]))
    box_slots = gather_blocks(received)
    return (surface, box_slots.reshape(1, 1, owners * capacity, -1))


def solution(mesh):
    return jax.shard_map(
        on_device,
        mesh=mesh,
        in_specs=(
            P("wide", "narrow", None),
            P(None, "wide", "narrow", None),
            P("wide", "narrow", None, None),
        ),
        out_specs=(P("wide", "narrow", None), P("wide", "narrow", None, None)),
        check_vma=False,
    )
```
